32 devices in a mesh: pb: 8 (over z, x), ka: 4 (over y, core).
Axes of the slice: x: 2, y: 2, z: 4, core: 2. Of those that a mesh axis runs over, the one named last changes fastest.
Arguments:
- node_states: float32 [512, 256], P('pb'), may hold values from -17 to 17
- frames: float32 [12, 512], P(None, 'pb'), may hold values from -20 to 20, as said below
- edge_states: bfloat16 [512, 512, 128], P('pb', 'ka'), may hold values from -6 to 6
- chain_number: int32 [512], replicated, may hold values from 0 to 3, as said below
- residue_index: int32 [512], replicated, may hold values from 0 to 767, as said below
- padding_mask: int32 [512], replicated, may hold values from 0 to 1, as said below
- query_weight: bfloat16 [256, 2048], replicated, may hold values from -0.375 to 0.375
- key_weight: bfloat16 [256, 2048], replicated, may hold values from -0.375 to 0.375
- value_weight: bfloat16 [256, 2048], replicated, may hold values from -0.375 to 0.375
- point_query: bfloat16 [256, 192], replicated, may hold values from -0.375 to 0.375
- point_key: bfloat16 [256, 192], replicated, may hold values from -0.375 to 0.375
- point_value: bfloat16 [256, 288], replicated, may hold values from -0.375 to 0.375
- bias_weight: bfloat16 [128, 8], replicated, may hold values from -0.5 to 0.5
- point_gamma: float32 [8], replicated, may hold values from 0.3 to 3
- relpos_table: float32 [128, 128], replicated, may hold values from -3 to 3
- output_weight: bfloat16 [3456, 256], replicated, may hold values from -0.109375 to 0.109375
- attention_scales: float32 [256], replicated, may hold values from 0.5 to 1.5
- layer_project: bfloat16 [2, 256, 768], replicated, may hold values from -0.375 to 0.375
- layer_output: bfloat16 [2, 256, 256], replicated, may hold values from -0.375 to 0.375
- layer_expand: bfloat16 [2, 256, 256], replicated, may hold values from -0.375 to 0.375
- layer_shrink: bfloat16 [2, 256, 256], replicated, may hold values from -0.375 to 0.375
- layer_scales: float32 [2, 2, 256], replicated, may hold values from 0.5 to 1.5
- frame_weight: float32 [256, 6], replicated, may hold values from -0.375 to 0.375
- node_to_edge: bfloat16 [256, 768], replicated, may hold values from -0.375 to 0.375
- edge_first: bfloat16 [128, 384], replicated, may hold values from -0.5 to 0.5
- edge_second: bfloat16 [384, 384], replicated, may hold values from -0.3125 to 0.3125
- edge_third: bfloat16 [384, 128], replicated, may hold values from -0.3125 to 0.3125
- edge_biases: float32 [2, 384], replicated, may hold values from -3 to 3
- edge_scales: float32 [128], replicated, may hold values from 0.5 to 1.5
Outputs:
- node_out: float32 [512, 256], P('pb')
- frames_out: float32 [12, 512], P(None, 'pb')
- edges_out: bfloat16 [512, 512, 128], P('pb', 'ka')
The draws below stay inside these ranges and needn't reach their ends.
Inputs may be any that keep to these rules, and one draw needn't show every extreme that they name: `chain_number`: never falls from one residue to the next; the first residue has 0 and the last 3. `residue_index`: rises by 1 or 2 from one residue to the next, starting at 0; exactly 256 of the rises are 2. `padding_mask`: the ones come first; at least 256 residues are ones and at least one is padding. `frames`: rows 0 to 8 form a proper rotation of each residue.
All inputs are finite; a program needn't handle non-finite values.
Results may differ from the reference program's by a relative error of at most 0.025.
Values may be sent and summed in bfloat16 or wider, within the bound.
A program may use at most 128 MiB of HBM per device.

```python
import math
import jax
import jax.numpy as jnp
from jax import lax

C_S = 256
C_Z = 128
HEADS = 8
HD = 256
QKP = 8
VP = 12
EH = 384
RELBINS = 128
LAYERS = 2
N = 512
QD = 64
TF_HD = 64
N_PB = 8


def draw_structure(key):
    position = jnp.arange(N, dtype=jnp.int32)
    bounds = jax.random.randint(jax.random.fold_in(key, 101), (3,), 1, N)
    chains = jnp.sum((position[:, None] >= bounds[None, :]).astype(jnp.int32), axis=1).astype(jnp.int32)
    order = jax.random.permutation(jax.random.fold_in(key, 102), N - 1)
    rises = (1 + (order < N // 2).astype(jnp.int32)).astype(jnp.int32)
    indices = jnp.concatenate([jnp.zeros((1,), jnp.int32), jnp.cumsum(rises).astype(jnp.int32)]).astype(jnp.int32)
    valid_count = jax.random.randint(jax.random.fold_in(key, 103), (), N // 2, N)
    masks = (position < valid_count).astype(jnp.int32)
    return (chains, indices, masks)


def draw_chain_number(key, part):
    return draw_structure(key)[0]


def draw_residue_index(key, part):
    return draw_structure(key)[1]


def draw_padding_mask(key, part):
    return draw_structure(key)[2]


def draw_node_states(key, part):
    value_key = jax.random.fold_in(key, 201)
    return jnp.clip(jax.random.normal(value_key, (N, C_S), jnp.float32), -6.0, 6.0)


def draw_frames(key, part):
    turns = jax.random.normal(jax.random.fold_in(key, 301), (4, N), jnp.float32)
    turns = turns / jnp.sqrt(jnp.sum(turns * turns, axis=0, keepdims=True) + 1e-12)
    real_part = turns[0]
    first_imag = turns[1]
    second_imag = turns[2]
    third_imag = turns[3]
    entries = jnp.stack([real_part * real_part + first_imag * first_imag - second_imag * second_imag - third_imag * third_imag, 2.0 * (first_imag * second_imag - real_part * third_imag), 2.0 * (first_imag * third_imag + real_part * second_imag), 2.0 * (first_imag * second_imag + real_part * third_imag), real_part * real_part - first_imag * first_imag + second_imag * second_imag - third_imag * third_imag, 2.0 * (second_imag * third_imag - real_part * first_imag), 2.0 * (first_imag * third_imag - real_part * second_imag), 2.0 * (second_imag * third_imag + real_part * first_imag), real_part * real_part - first_imag * first_imag - second_imag * second_imag + third_imag * third_imag], axis=0)
    shifts = jnp.clip(jax.random.normal(jax.random.fold_in(key, 302), (3, N), jnp.float32), -4.0, 4.0)
    return jnp.concatenate([entries, shifts], axis=0)


def block_levels(own_key, shape, pieces, smallest, top_value):
    level = 1.0
    for dim, shards_of in pieces:
        heights = jax.random.uniform(jax.random.fold_in(jax.random.fold_in(own_key, 6), dim), (shards_of,), jnp.float32, smallest / len(pieces), top_value / len(pieces))
        level = level * jnp.repeat(jnp.exp(heights), shape[dim] // shards_of).reshape((-1,) + (1,) * (len(shape) - 1 - dim))
    return level


def noise(key, dims, spread, limit, split=(), held_as=jnp.bfloat16):
    level = block_levels(key, dims, split, -0.22, 0.18) if split else 1.0
    values = jax.random.normal(key, dims, jnp.float32) * spread * level
    return jnp.minimum(jnp.maximum(values, -limit), limit).astype(held_as)


def setup_inputs(seed: int = 0) -> dict:
    keys = jax.random.split(jax.random.key(seed), 30)
    node_states = draw_node_states(jax.random.fold_in(keys[29], 71), 0)
    frames = draw_frames(jax.random.fold_in(keys[29], 71), 0)
    edge_states = noise(keys[2], (N, N, C_Z), 1.0, 6.0, ((0, 8), (1, 4)))
    chain_number = draw_chain_number(jax.random.fold_in(keys[29], 71), 0)
    residue_index = draw_residue_index(jax.random.fold_in(keys[29], 71), 0)
    padding_mask = draw_padding_mask(jax.random.fold_in(keys[29], 71), 0)
    query_weight = noise(keys[6], (C_S, HEADS * HD), C_S ** -0.5, 0.375)
    key_weight = noise(keys[7], (C_S, HEADS * HD), C_S ** -0.5, 0.375)
    value_weight = noise(keys[8], (C_S, HEADS * HD), C_S ** -0.5, 0.375)
    point_query = noise(keys[9], (C_S, HEADS * 3 * QKP), C_S ** -0.5, 0.375)
    point_key = noise(keys[10], (C_S, HEADS * 3 * QKP), C_S ** -0.5, 0.375)
    point_value = noise(keys[11], (C_S, HEADS * 3 * VP), C_S ** -0.5, 0.375)
    bias_weight = noise(keys[12], (C_Z, HEADS), C_Z ** -0.5, 0.5)
    point_gamma = jnp.clip(jnp.exp(jax.random.uniform(keys[13], (HEADS,), jnp.float32, math.log(0.3), math.log(3.0))), 0.3, 3.0)
    relpos_table = noise(keys[14], (RELBINS, C_Z), 0.5, 3.0, (), jnp.float32)
    output_weight = noise(keys[15], (HEADS * (HD + C_Z + 4 * VP), C_S), (HEADS * (HD + C_Z + 4 * VP)) ** -0.5, 0.109375)
    attention_scales = jnp.clip(1.0 + 0.1 * jax.random.normal(keys[16], (C_S,), jnp.float32), 0.5, 1.5)
    layer_project = noise(keys[17], (LAYERS, C_S, 3 * C_S), C_S ** -0.5, 0.375)
    layer_output = noise(keys[18], (LAYERS, C_S, C_S), C_S ** -0.5, 0.375)
    layer_expand = noise(keys[19], (LAYERS, C_S, C_S), C_S ** -0.5, 0.375)
    layer_shrink = noise(keys[20], (LAYERS, C_S, C_S), C_S ** -0.5, 0.375)
    layer_scales = jnp.clip(1.0 + 0.1 * jax.random.normal(keys[21], (LAYERS, 2, C_S), jnp.float32), 0.5, 1.5)
    frame_weight = noise(keys[22], (C_S, 6), C_S ** -0.5, 0.375, (), jnp.float32)
    node_to_edge = noise(keys[23], (C_S, 2 * EH), C_S ** -0.5, 0.375)
    edge_first = noise(keys[24], (C_Z, EH), C_Z ** -0.5, 0.5)
    edge_second = noise(keys[25], (EH, EH), EH ** -0.5, 0.3125)
    edge_third = noise(keys[26], (EH, C_Z), EH ** -0.5, 0.3125)
    edge_biases = noise(keys[27], (2, EH), 0.5, 3.0, (), jnp.float32)
    edge_scales = jnp.clip(1.0 + 0.1 * jax.random.normal(keys[28], (C_Z,), jnp.float32), 0.5, 1.5)
    return dict(node_states=node_states, frames=frames, edge_states=edge_states, chain_number=chain_number, residue_index=residue_index, padding_mask=padding_mask, query_weight=query_weight, key_weight=key_weight, value_weight=value_weight, point_query=point_query, point_key=point_key, point_value=point_value, bias_weight=bias_weight, point_gamma=point_gamma, relpos_table=relpos_table, output_weight=output_weight, attention_scales=attention_scales, layer_project=layer_project, layer_output=layer_output, layer_expand=layer_expand, layer_shrink=layer_shrink, layer_scales=layer_scales, frame_weight=frame_weight, node_to_edge=node_to_edge, edge_first=edge_first, edge_second=edge_second, edge_third=edge_third, edge_biases=edge_biases, edge_scales=edge_scales)


HIGHEST = lax.Precision.HIGHEST
NEG_FILL = -1000000000.0

def layer_norm(values, scales):
    centered = values - lax.optimization_barrier(jnp.mean(values, axis=-1, keepdims=True))
    variance = lax.optimization_barrier(jnp.mean(centered * centered, axis=-1, keepdims=True))
    return centered * lax.rsqrt(variance + 1e-05) * scales

def frame_parts(frames):
    rotation = jnp.transpose(frames[:9]).reshape(-1, 3, 3)
    offset = jnp.transpose(frames[9:12])
    return (rotation, offset)

def head_split(matrix, width):
    return matrix.reshape(matrix.shape[0], -1, width)

def place_points(features, weight, rotation, offset, count):
    local = jnp.dot(features, weight, preferred_element_type=jnp.float32)
    local = local.reshape(local.shape[0], HEADS, 3, count)
    placed = jnp.einsum('rcd,rhdp->rhcp', rotation, local, precision=HIGHEST)
    return placed + offset[:, None, :, None]

def relative_bins(chain_rows, index_rows, chain_cols, index_cols):
    reach = (RELBINS - 2) // 2
    gap_class = jnp.clip(index_rows[:, None] - index_cols[None, :], -reach, reach) + reach
    same_chain = chain_rows[:, None] == chain_cols[None, :]
    return jnp.where(same_chain, gap_class, RELBINS - 1).astype(jnp.int32)

def point_logits(queries, key_vectors, query_places, key_places, pair_rep, bias_weight, point_gamma):
    scalar = jnp.einsum('ihd,jhd->hij', queries.astype(jnp.float32), key_vectors.astype(jnp.float32), precision=HIGHEST) / math.sqrt(HD)
    pair_bias = jnp.einsum('ijc,ch->hij', pair_rep.astype(jnp.float32), bias_weight.astype(jnp.float32), precision=HIGHEST)
    query_square = lax.optimization_barrier(jnp.sum(query_places * query_places, axis=(2, 3)))
    key_square = lax.optimization_barrier(jnp.sum(key_places * key_places, axis=(2, 3)))
    cross = jnp.einsum('ihcp,jhcp->hij', query_places, key_places, precision=HIGHEST)
    distance = jnp.transpose(query_square)[:, :, None] + jnp.transpose(key_square)[:, None, :] - 2.0 * cross
    weight_points = math.sqrt(2.0 / (9.0 * QKP))
    return math.sqrt(1.0 / 3.0) * (scalar + pair_bias - 0.5 * weight_points * point_gamma[:, None, None] * distance)

def ipa_features(scalar_out, pair_out, point_global, rotation, offset):
    moved = point_global - offset[:, None, :, None]
    local = jnp.einsum('icd,ihcp->ihdp', rotation, moved, precision=HIGHEST)
    lengths = jnp.sqrt(lax.optimization_barrier(jnp.sum(local * local, axis=2)) + 1e-08)
    count = scalar_out.shape[0]
    return jnp.concatenate([scalar_out.reshape(count, -1), pair_out.reshape(count, -1), local.reshape(count, -1), lengths.reshape(count, -1)], axis=1)

def encoder_core(states, query_half, key_value, valid, output, expand, shrink, scales):
    queries = head_split(query_half, TF_HD)
    key_vectors = head_split(key_value[:, :C_S], TF_HD)
    value_vectors = head_split(key_value[:, C_S:], TF_HD)
    scores = jnp.einsum('ihd,jhd->hij', queries.astype(jnp.float32), key_vectors.astype(jnp.float32), precision=HIGHEST) / math.sqrt(TF_HD)
    masked = jnp.where(valid[None, None, :], scores, NEG_FILL)
    row_top = lax.optimization_barrier(jnp.max(masked, axis=-1, keepdims=True))
    weights = jnp.where(valid[None, None, :], jnp.exp(masked - row_top), 0.0)
    attention = (weights / lax.optimization_barrier(jnp.sum(weights, axis=-1, keepdims=True))).astype(jnp.bfloat16)
    context = jnp.einsum('hij,jhd->ihd', attention.astype(jnp.float32), value_vectors.astype(jnp.float32), precision=HIGHEST).astype(jnp.bfloat16)
    context = context.reshape(states.shape[0], C_S)
    middle = layer_norm(states + jnp.dot(context, output, preferred_element_type=jnp.float32), scales[0])
    hidden = jax.nn.relu(jnp.dot(middle.astype(jnp.bfloat16), expand, preferred_element_type=jnp.float32)).astype(jnp.bfloat16)
    return layer_norm(middle + jnp.dot(hidden, shrink, preferred_element_type=jnp.float32), scales[1])

def update_frames(states, frames, frame_weight):
    update = jnp.dot(states, frame_weight, precision=HIGHEST)
    length = jnp.sqrt(1.0 + update[:, 0] * update[:, 0] + update[:, 1] * update[:, 1] + update[:, 2] * update[:, 2])
    real_part = 1.0 / length
    first_imag = update[:, 0] / length
    second_imag = update[:, 1] / length
    third_imag = update[:, 2] / length
    row_one = jnp.stack([real_part * real_part + first_imag * first_imag - second_imag * second_imag - third_imag * third_imag, 2.0 * (first_imag * second_imag - real_part * third_imag), 2.0 * (first_imag * third_imag + real_part * second_imag)], axis=1)
    row_two = jnp.stack([2.0 * (first_imag * second_imag + real_part * third_imag), real_part * real_part - first_imag * first_imag + second_imag * second_imag - third_imag * third_imag, 2.0 * (second_imag * third_imag - real_part * first_imag)], axis=1)
    row_three = jnp.stack([2.0 * (first_imag * third_imag - real_part * second_imag), 2.0 * (second_imag * third_imag + real_part * first_imag), real_part * real_part - first_imag * first_imag - second_imag * second_imag + third_imag * third_imag], axis=1)
    turn = jnp.stack([row_one, row_two, row_three], axis=1)
    rotation, offset = frame_parts(frames)
    new_rotation = jnp.einsum('rcd,rde->rce', rotation, turn, precision=HIGHEST)
    new_offset = jnp.einsum('rcd,rd->rc', rotation, update[:, 3:6], precision=HIGHEST) + offset
    return jnp.transpose(jnp.concatenate([new_rotation.reshape(-1, 9), new_offset], axis=1))

def rows_of(array, row_first):
    return lax.dynamic_slice_in_dim(array, row_first, QD, 0)

def reference(node_states, frames, edge_states, chain_number, residue_index, padding_mask, query_weight, key_weight, value_weight, point_query, point_key, point_value, bias_weight, point_gamma, relpos_table, output_weight, attention_scales, layer_project, layer_output, layer_expand, layer_shrink, layer_scales, frame_weight, node_to_edge, edge_first, edge_second, edge_third, edge_biases, edge_scales):
    rotation, offset = frame_parts(frames)
    rounded = node_states.astype(jnp.bfloat16)
    queries = head_split(jnp.dot(rounded, query_weight, preferred_element_type=jnp.float32).astype(jnp.bfloat16), HD)
    key_vectors = head_split(jnp.dot(rounded, key_weight, preferred_element_type=jnp.float32).astype(jnp.bfloat16), HD)
    value_vectors = head_split(jnp.dot(rounded, value_weight, preferred_element_type=jnp.float32).astype(jnp.bfloat16), HD)
    query_places = place_points(rounded, point_query, rotation, offset, QKP)
    key_places = place_points(rounded, point_key, rotation, offset, QKP)
    value_places = place_points(rounded, point_value, rotation, offset, VP)
    valid = padding_mask == 1
    live_float = valid.astype(jnp.float32)
    starts = jnp.arange(N_PB, dtype=jnp.int32) * QD

    def pair_rows(row_first):
        edge_rows = rows_of(edge_states, row_first)
        bins = relative_bins(rows_of(chain_number, row_first), rows_of(residue_index, row_first), chain_number, residue_index)
        relative = jnp.take(relpos_table, bins, axis=0)
        return (edge_rows.astype(jnp.float32) + relative).astype(jnp.bfloat16)

    def attend_rows(row_first):
        pair_rep = pair_rows(row_first)
        logits = point_logits(rows_of(queries, row_first), key_vectors, rows_of(query_places, row_first), key_places, pair_rep, bias_weight, point_gamma)
        masked = jnp.where(valid[None, None, :], logits, NEG_FILL)
        row_top = lax.optimization_barrier(jnp.max(masked, axis=-1, keepdims=True))
        weights = jnp.where(valid[None, None, :], jnp.exp(masked - row_top), 0.0)
        attention = weights / lax.optimization_barrier(jnp.sum(weights, axis=-1, keepdims=True))
        scalar_out = jnp.einsum('hij,jhd->ihd', attention, value_vectors.astype(jnp.float32), precision=HIGHEST)
        pair_out = jnp.einsum('hij,ijc->ihc', attention, pair_rep.astype(jnp.float32), precision=HIGHEST)
        point_global = jnp.einsum('hij,jhcp->ihcp', attention, value_places, precision=HIGHEST)
        return ipa_features(scalar_out, pair_out, point_global, rows_of(rotation, row_first), rows_of(offset, row_first))
    features = lax.map(attend_rows, starts)
    features = features.reshape(N, -1).astype(jnp.bfloat16)
    states = layer_norm(node_states + jnp.dot(features, output_weight, preferred_element_type=jnp.float32), attention_scales)
    for layer_number in range(LAYERS):
        projected = jnp.dot(states.astype(jnp.bfloat16), layer_project[layer_number], preferred_element_type=jnp.float32).astype(jnp.bfloat16)
        states = encoder_core(states, projected[:, :C_S], projected[:, C_S:], valid, layer_output[layer_number], layer_expand[layer_number], layer_shrink[layer_number], layer_scales[layer_number])
    frames_out = update_frames(states, frames, frame_weight)
    edge_projection = jnp.dot(states.astype(jnp.bfloat16), node_to_edge, preferred_element_type=jnp.float32)

    def edge_rows_update(row_first):
        pair_rep = pair_rows(row_first)
        query_part = rows_of(edge_projection, row_first)[:, :EH]
        hidden = jnp.dot(pair_rep.reshape(-1, C_Z), edge_first, preferred_element_type=jnp.float32).reshape(QD, N, EH)
        hidden = jax.nn.relu(hidden + query_part[:, None, :] + edge_projection[None, :, EH:] + edge_biases[0]).astype(jnp.bfloat16)
        middle = jax.nn.relu(jnp.dot(hidden.reshape(-1, EH), edge_second, preferred_element_type=jnp.float32) + edge_biases[1]).astype(jnp.bfloat16)
        result = pair_rep.astype(jnp.float32) + jnp.dot(middle, edge_third, preferred_element_type=jnp.float32).reshape(QD, N, C_Z)
        live = rows_of(live_float, row_first)[:, None, None] * live_float[None, :, None]
        return (layer_norm(result, edge_scales) * live).astype(jnp.bfloat16)
    edges_out = lax.map(edge_rows_update, starts).reshape(N, N, C_Z)
    return (states, frames_out, edges_out)
```

```python
import functools
import math

import jax
import jax.numpy as jnp
import numpy as np
from jax import lax
from jax.experimental import pallas as pl
from jax.experimental.pallas import tpu as pltpu
from jax.sharding import PartitionSpec as P

C_S = 256
C_Z = 128
HEADS = 8
HD = 256
QKP = 8
VP = 12
EH = 384
RELBINS = 128
LAYERS = 2
TF_HD = 64
LANES = 128

HIGHEST = lax.Precision.HIGHEST
NEG_FILL = -1000000000.0
CHAIN_STEP = 65536.0
MESH = pl.DeviceIdType.MESH
VMEM = pl.BlockSpec(memory_space=pltpu.VMEM)
ANY = pl.BlockSpec(memory_space=pl.ANY)


def dot(a, b, **options):
    return jnp.dot(a, b, preferred_element_type=jnp.float32, **options)


def contract(a, b, a_dim, b_dim, **options):
    return lax.dot_general(
        a, b, (((a_dim,), (b_dim,)), ((), ())), preferred_element_type=jnp.float32, **options
    )


def iota(shape, dim):
    return lax.broadcasted_iota(jnp.int32, shape, dim)


def layer_norm(values, scales):
    centered = values - jnp.mean(values, axis=-1, keepdims=True)
    variance = jnp.mean(centered * centered, axis=-1, keepdims=True)
    return centered * lax.rsqrt(variance + 1e-05) * scales


def by_component(count):
    target = np.arange(3 * LANES)
    comp, rest = target // LANES, target % LANES
    source = (rest // count * 3 + comp) * count + rest % count
    source = np.where(rest < HEADS * count, source, -1)
    return np.arange(HEADS * 3 * count)[:, None] == source[None, :]


def frame_columns(frames):
    count = frames.shape[0]
    eye = (iota((count, LANES), 0) == iota((count, LANES), 1)).astype(jnp.float32)
    return contract(frames, eye, 0, 0, precision=HIGHEST)


def place(local, columns):
    parts = [local[:, LANES * d : LANES * (d + 1)] for d in range(3)]
    return jnp.concatenate(
        [
            sum(columns[:, 3 * c + d : 3 * c + d + 1] * parts[d] for d in range(3))
            + columns[:, 9 + c : 10 + c]
            for c in range(3)
        ],
        axis=1,
    )


def head_of_lane(count):
    lane = iota((HEADS, 3 * LANES), 1) % LANES
    return (lane // count == iota((HEADS, 3 * LANES), 0)).astype(jnp.float32)


def attend_kernel(
    n_pb,
    n_ka,
    node,
    frames,
    chain,
    index,
    mask,
    point_query,
    point_key,
    point_value,
    bias_weight,
    gamma,
    relpos,
    scales,
    perm_qk,
    perm_v,
    perm_vt,
    first,
    edge_hbm,
    wq_hbm,
    wk_hbm,
    wv_hbm,
    ow_hbm,
    states_out,
    pair_hbm,
    hidden_hbm,
    edge_s,
    pair_s,
    hidden_s,
    wq,
    wk,
    wv,
    ow,
    x_send,
    x_keys,
    f_keys,
    bias_s,
    work_s,
    stats_send,
    stats_recv,
    part_send,
    part_recv,
    columns_s,
    node_s,
    mine,
    load_sem,
    store_sem,
    x_send_sem,
    x_recv_sem,
    f_send_sem,
    f_recv_sem,
    s_send_sem,
    s_recv_sem,
    p_send_sem,
    p_recv_sem,
    g_send_sem,
    g_recv_sem,
    h_send_sem,
    h_recv_sem,
):
    rows, keys, channels = edge_s.shape
    count = chain.shape[1]
    part = rows // n_ka
    per = n_pb // n_ka
    row, col = lax.axis_index("pb"), lax.axis_index("ka")
    along_pb = [{"pb": lax.rem(row + d, n_pb)} for d in range(1, n_pb)]
    others = [lax.rem(col + d, n_ka) for d in range(1, n_ka)]
    along_ka = [{"ka": other} for other in others]

    barrier = pltpu.get_barrier_semaphore()
    for peer in along_pb + along_ka:
        pl.semaphore_signal(barrier, inc=1, device_id=peer, device_id_type=MESH)
    loads = [
        pltpu.make_async_copy(source, target, load_sem.at[k])
        for k, (source, target) in enumerate(
            ((edge_hbm, edge_s), (wq_hbm, wq), (wk_hbm, wk), (wv_hbm, wv), (ow_hbm, ow))
        )
    ]
    for load in loads:
        load.start()

    x_send[...] = node[...].astype(jnp.bfloat16)

    code = chain[...].astype(jnp.float32) * CHAIN_STEP + index[...].astype(jnp.float32)
    code = jnp.broadcast_to(code, (8, count))
    at_row = iota((count, LANES), 0) == row * rows + iota((count, LANES), 1)
    row_code = dot(code, at_row.astype(jnp.float32), precision=HIGHEST)[0:1]
    at_key = iota((keys, count), 1) == col * keys + iota((keys, count), 0)
    key_code = contract(at_key.astype(jnp.float32), code, 1, 1, precision=HIGHEST)[:, 0:1]
    reach = (RELBINS - 2) // 2
    gap = row_code - key_code
    bins = jnp.where(
        jnp.abs(gap) < CHAIN_STEP / 2, jnp.clip(gap, -reach, reach) + reach, RELBINS - 1.0
    )
    table = relpos[...]
    high = table.astype(jnp.bfloat16)
    low = (table - high.astype(jnp.float32)).astype(jnp.bfloat16)
    table = jnp.concatenate([high, low], axis=1)
    bin_lane = iota((keys, RELBINS), 1).astype(jnp.float32)
    eye = (iota((channels, channels), 0) == iota((channels, channels), 1)).astype(jnp.bfloat16)
    bias_rows = contract(bias_weight[...], eye, 0, 0).astype(jnp.bfloat16)
    loads[0].wait()

    def pair_rows(start, size):
        onehot = jnp.concatenate(
            [
                jnp.where(bins[:, i : i + 1] == bin_lane, 1.0, 0.0).astype(jnp.bfloat16)
                for i in range(start, start + size)
            ],
            axis=0,
        )
        relative = dot(onehot, table)
        relative = relative[:, :channels] + relative[:, channels:]
        values = edge_s[start : start + size].astype(jnp.float32).reshape(size * keys, channels)
        values = (values + relative).astype(jnp.bfloat16)
        pair_s[start : start + size] = values.reshape(size, keys, channels)
        for i in range(size):
            bias_s[(start + i) * HEADS : (start + i + 1) * HEADS, :] = contract(
                bias_rows, values[i * keys : (i + 1) * keys], 1, 1
            )

    group = 8
    starts = list(range(0, rows, group))
    early = starts[: len(starts) // 2]
    late = starts[len(starts) // 2 :]
    for start in early:
        pair_rows(start, group)

    pl.semaphore_wait(barrier, len(along_pb) + len(along_ka))
    for slot in range(per):

        @pl.when(row == col * per + slot)
        def _():
            copies = []
            for d, peer in enumerate(along_pb):
                copies.append(
                    pltpu.make_async_remote_copy(
                        src_ref=x_send,
                        dst_ref=x_keys.at[slot],
                        send_sem=x_send_sem.at[d],
                        recv_sem=x_recv_sem.at[slot],
                        device_id=peer,
                        device_id_type=MESH,
                    )
                )
                copies.append(
                    pltpu.make_async_remote_copy(
                        src_ref=frames,
                        dst_ref=f_keys.at[slot],
                        send_sem=f_send_sem.at[d],
                        recv_sem=f_recv_sem.at[slot],
                        device_id=peer,
                        device_id_type=MESH,
                    )
                )
            for copy in copies:
                copy.start()
            x_keys[slot] = x_send[...]
            f_keys[slot] = frames[...]

    for start in late:
        pair_rows(start, group)
    pair_store = pltpu.make_async_copy(pair_s, pair_hbm, store_sem.at[0])
    pair_store.start()

    own_columns = frame_columns(frames[...])
    for a in range(n_ka):
        columns_s[a] = own_columns[a * part : (a + 1) * part]
        node_s[a] = node[a * part : (a + 1) * part, :]
    own = x_send[...]
    loads[1].wait()
    queries = dot(own, wq[...]).astype(jnp.bfloat16)
    spread = dot(point_query[...], perm_qk[...]).astype(jnp.bfloat16)
    query_places = place(dot(own, spread), own_columns)
    spread_key = dot(point_key[...], perm_qk[...]).astype(jnp.bfloat16)
    spread_value = dot(point_value[...], perm_v[...]).astype(jnp.bfloat16)
    heads_qk = head_of_lane(QKP)
    by_head = (query_places[:, None, :] * heads_qk[None]).reshape(rows * HEADS, 3 * LANES)
    query_square = jnp.sum(by_head * by_head, axis=-1, keepdims=True)

    for slot in range(per):

        @pl.when(row != col * per + slot)
        def _():
            pltpu.make_async_remote_copy(
                src_ref=x_send,
                dst_ref=x_keys.at[slot],
                send_sem=x_send_sem.at[0],
                recv_sem=x_recv_sem.at[slot],
                device_id=along_pb[0],
                device_id_type=MESH,
            ).wait_recv()
            pltpu.make_async_remote_copy(
                src_ref=frames,
                dst_ref=f_keys.at[slot],
                send_sem=f_send_sem.at[0],
                recv_sem=f_recv_sem.at[slot],
                device_id=along_pb[0],
                device_id_type=MESH,
            ).wait_recv()

    key_rows = jnp.concatenate([x_keys[slot] for slot in range(per)], axis=0)
    key_columns = jnp.concatenate([frame_columns(f_keys[slot]) for slot in range(per)], axis=0)
    key_places = place(dot(key_rows, spread_key), key_columns)
    cross = contract(by_head, key_places, 1, 1, precision=HIGHEST)
    key_square = contract(heads_qk, key_places * key_places, 1, 1, precision=HIGHEST)
    loads[2].wait()
    key_vectors = dot(key_rows, wk[...]).astype(jnp.bfloat16)
    for head in range(HEADS):
        window = slice(head * HD, (head + 1) * HD)
        work_s[pl.ds(head, rows, stride=HEADS), :] = contract(
            queries[:, window], key_vectors[:, window], 1, 1
        )
    own_head = iota((HEADS, HEADS), 0) == iota((HEADS, HEADS), 1)
    gammas = jnp.sum(jnp.where(own_head, gamma[...], 0.0), axis=1, keepdims=True)
    gammas = gammas * math.sqrt(2.0 / (9.0 * QKP))
    distance = (cross - 0.5 * query_square).reshape(rows, HEADS, keys) - 0.5 * key_square[None]
    logits = math.sqrt(1.0 / 3.0) * (
        work_s[...].reshape(rows, HEADS, keys) * (1.0 / math.sqrt(HD))
        + bias_s[...].reshape(rows, HEADS, keys)
        + gammas[None] * distance
    )
    key_first = pl.multiple_of(col * keys, keys)
    valid = (mask[0:1, pl.ds(key_first, keys)] == 1)[None]
    masked = jnp.where(valid, logits, NEG_FILL)
    top = jnp.max(masked, axis=-1, keepdims=True)
    weights = jnp.where(valid, jnp.exp(masked - top), 0.0)
    total = jnp.sum(weights, axis=-1, keepdims=True)
    lanes = stats_send.shape[-1]
    at_lane = iota((rows, 1, lanes), 0) == iota((rows, 1, lanes), 2)
    stats_send[0] = jnp.sum(jnp.where(at_lane, top, 0.0), axis=0)
    stats_send[1] = jnp.sum(jnp.where(at_lane, total, 0.0), axis=0)
    stats = [
        pltpu.make_async_remote_copy(
            src_ref=stats_send,
            dst_ref=stats_recv.at[d],
            send_sem=s_send_sem.at[d],
            recv_sem=s_recv_sem.at[d],
            device_id=peer,
            device_id_type=MESH,
        )
        for d, peer in enumerate(along_ka)
    ]
    for copy in stats:
        copy.start()

    work_s[...] = weights.reshape(rows * HEADS, keys)
    rounded = weights.astype(jnp.bfloat16)
    loads[3].wait()
    value_vectors = dot(key_rows, wv[...]).astype(jnp.bfloat16)
    scalar = [
        dot(
            work_s[pl.ds(head, rows, stride=HEADS), :].astype(jnp.bfloat16),
            value_vectors[:, head * HD : (head + 1) * HD],
        )
        for head in range(HEADS)
    ]
    pair_out = jnp.stack([dot(rounded[i], pair_s[i]) for i in range(rows)], axis=0)
    value_places = place(dot(key_rows, spread_value), key_columns)
    heads_v = head_of_lane(VP)
    points = dot(weights.reshape(rows * HEADS, keys), value_places, precision=HIGHEST)

    for copy in stats:
        copy.wait()
    highest = stats_send[0]
    for d in range(n_ka - 1):
        highest = jnp.maximum(highest, stats_recv[d, 0])
    share = jnp.exp(stats_send[0] - highest)
    whole = stats_send[1] * share
    for d in range(n_ka - 1):
        whole = whole + stats_recv[d, 1] * jnp.exp(stats_recv[d, 0] - highest)
    real_row = iota(whole.shape, 1) < rows
    share = jnp.where(real_row, share / jnp.where(real_row, whole, 1.0), 0.0)
    factor = jnp.sum(jnp.where(at_lane, share[None], 0.0), axis=-1, keepdims=True)
    bias_s[...] = jnp.broadcast_to(factor, (rows, HEADS, keys)).reshape(rows * HEADS, keys)
    work_s[...] = (pair_out * factor).reshape(rows * HEADS, channels)
    loads[4].wait()
    features = []
    for head in range(HEADS):
        scale = bias_s[pl.ds(head, rows, stride=HEADS), :]
        for half in range(HD // LANES):
            features.append(scalar[head][:, half * LANES : (half + 1) * LANES] * scale)
    for head in range(HEADS):
        features.append(work_s[pl.ds(head, rows, stride=HEADS), :])
    features = jnp.concatenate([piece.astype(jnp.bfloat16) for piece in features], axis=1)
    partial = dot(features, ow[: features.shape[1], :])
    points = points.reshape(rows, HEADS, 3 * LANES) * (heads_v[None] * factor)
    points = jnp.sum(points, axis=1)
    partial = jnp.concatenate([partial, points], axis=1)
    for a in range(n_ka):
        part_send[a] = partial[a * part : (a + 1) * part].astype(jnp.bfloat16)
    parts = [
        pltpu.make_async_remote_copy(
            src_ref=part_send.at[other],
            dst_ref=part_recv.at[d],
            send_sem=p_send_sem.at[d],
            recv_sem=p_recv_sem.at[d],
            device_id={"ka": other},
            device_id_type=MESH,
        )
        for d, other in enumerate(others)
    ]
    for copy in parts:
        copy.start()

    def hidden_rows(start):
        pair = pair_s[start : start + group].reshape(group * keys, channels)
        values = dot(pair, first[...]).astype(jnp.bfloat16)
        hidden_s[start : start + group] = values.reshape(group, keys, EH)
        store = pltpu.make_async_copy(
            hidden_s.at[pl.ds(start, group)],
            hidden_hbm.at[pl.ds(start, group)],
            store_sem.at[1 + start // group],
        )
        store.start()
        return store

    third = -(-len(starts) // 3)
    stores = [hidden_rows(start) for start in starts[:third]]
    value_base = HEADS * (HD + C_Z)
    point_weight = dot(perm_vt[...], ow[value_base : value_base + HEADS * 3 * VP, :]).astype(
        jnp.bfloat16
    )
    for copy in parts:
        copy.wait()
    merged = part_send[col].astype(jnp.float32)
    for d in range(n_ka - 1):
        merged = merged + part_recv[d].astype(jnp.float32)
    columns = columns_s[col]
    moved = [
        merged[:, C_S + LANES * c : C_S + LANES * (c + 1)] - columns[:, 9 + c : 10 + c]
        for c in range(3)
    ]
    local = [
        sum(columns[:, 3 * c + d : 3 * c + d + 1] * moved[c] for c in range(3)) for d in range(3)
    ]
    lengths = jnp.sqrt(sum(piece * piece for piece in local) + 1e-08)
    local = jnp.concatenate([piece.astype(jnp.bfloat16) for piece in local], axis=1)
    length_weight = ow[value_base + HEADS * 3 * VP :, :]
    states = (
        node_s[col]
        + merged[:, :C_S]
        + dot(local, point_weight)
        + dot(lengths[:, : HEADS * VP].astype(jnp.bfloat16), length_weight)
    )
    mine[...] = layer_norm(states, scales[...]).astype(jnp.bfloat16)
    states_out[row, col] = mine[...]
    gathers = [
        pltpu.make_async_remote_copy(
            src_ref=mine,
            dst_ref=states_out.at[row, col],
            send_sem=g_send_sem.at[d],
            recv_sem=g_recv_sem.at[d],
            device_id=peer,
            device_id_type=MESH,
        )
        for d, peer in enumerate(along_pb)
    ]
    for copy in gathers:
        copy.start()
    stores += [hidden_rows(start) for start in starts[third : 2 * third]]
    for copy in gathers:
        copy.wait()
    spreads = [
        pltpu.make_async_remote_copy(
            src_ref=states_out.at[:, col],
            dst_ref=states_out.at[:, col],
            send_sem=h_send_sem.at[d],
            recv_sem=h_recv_sem.at[d],
            device_id=peer,
            device_id_type=MESH,
        )
        for d, peer in enumerate(along_ka)
    ]
    for copy in spreads:
        copy.start()
    stores += [hidden_rows(start) for start in starts[2 * third :]]
    for slot in range(per):

        @pl.when(row == col * per + slot)
        def _():
            for d, peer in enumerate(along_pb):
                pltpu.make_async_remote_copy(
                    src_ref=x_send,
                    dst_ref=x_keys.at[slot],
                    send_sem=x_send_sem.at[d],
                    recv_sem=x_recv_sem.at[slot],
                    device_id=peer,
                    device_id_type=MESH,
                ).wait_send()
                pltpu.make_async_remote_copy(
                    src_ref=frames,
                    dst_ref=f_keys.at[slot],
                    send_sem=f_send_sem.at[d],
                    recv_sem=f_recv_sem.at[slot],
                    device_id=peer,
                    device_id_type=MESH,
                ).wait_send()

    for copy in spreads:
        copy.wait()
    pair_store.wait()
    for store in stores:
        store.wait()


def attend(n_pb, n_ka, small, large):
    node, frames, edge = small[0], small[1], large[0]
    rows, keys, channels = edge.shape
    part, per = rows // n_ka, n_pb // n_ka
    lanes = -(-rows // LANES) * LANES
    bf16, f32 = jnp.bfloat16, jnp.float32
    dma = pltpu.SemaphoreType.DMA
    return pl.pallas_call(
        functools.partial(attend_kernel, n_pb, n_ka),
        out_shape=(
            jax.ShapeDtypeStruct((n_pb, n_ka, part, C_S), bf16),
            jax.ShapeDtypeStruct(edge.shape, bf16),
            jax.ShapeDtypeStruct((rows, keys, EH), bf16),
        ),
        in_specs=[VMEM] * len(small) + [ANY] * len(large),
        out_specs=(VMEM, ANY, ANY),
        scratch_shapes=[
            pltpu.VMEM(edge.shape, bf16),
            pltpu.VMEM(edge.shape, bf16),
            pltpu.VMEM((rows, keys, EH), bf16),
            *[pltpu.VMEM(array.shape, bf16) for array in large[1:]],
            pltpu.VMEM((rows, C_S), bf16),
            pltpu.VMEM((per, rows, C_S), bf16),
            pltpu.VMEM((per,) + frames.shape, f32),
            pltpu.VMEM((rows * HEADS, keys), f32),
            pltpu.VMEM((rows * HEADS, keys), f32),
            pltpu.VMEM((2, HEADS, lanes), f32),
            pltpu.VMEM((n_ka - 1, 2, HEADS, lanes), f32),
            pltpu.VMEM((n_ka, part, C_S + 3 * LANES), bf16),
            pltpu.VMEM((n_ka - 1, part, C_S + 3 * LANES), bf16),
            pltpu.VMEM((n_ka, part, LANES), f32),
            pltpu.VMEM((n_ka, part, C_S), f32),
            pltpu.VMEM((part, C_S), bf16),
            dma((len(large),)),
            dma((1 + rows // 8,)),
            dma((n_pb - 1,)),
            dma((per,)),
            dma((n_pb - 1,)),
            dma((per,)),
            dma((n_ka - 1,)),
            dma((n_ka - 1,)),
            dma((n_ka - 1,)),
            dma((n_ka - 1,)),
            dma((n_pb - 1,)),
            dma((n_pb - 1,)),
            dma((n_ka - 1,)),
            dma((n_ka - 1,)),
        ],
        compiler_params=pltpu.CompilerParams(
            collective_id=0, has_side_effects=True, vmem_limit_bytes=40 << 20
        ),
    )(*small, *large)


def encoder_rows(states, key_value, fill, project, output, expand, shrink, scales):
    queries = dot(states.astype(jnp.bfloat16), project[:, :C_S]).astype(
        jnp.bfloat16
    ) * jnp.asarray(1.0 / math.sqrt(TF_HD), jnp.bfloat16)
    owner = iota((1, C_S), 1) // TF_HD
    context = jnp.zeros(states.shape, jnp.float32)
    for head in range(C_S // TF_HD):
        only = jnp.where(owner == head, 1.0, 0.0)
        scores = contract(queries * only.astype(jnp.bfloat16), key_value[:, :C_S], 1, 1) + fill
        weights = jnp.exp(scores - jnp.max(scores, axis=-1, keepdims=True))
        inverse = 1.0 / jnp.sum(weights, axis=-1, keepdims=True)
        mixed = dot(weights.astype(jnp.bfloat16), key_value[:, C_S:])
        context = context + mixed * (inverse * only)
    middle = layer_norm(states + dot(context.astype(jnp.bfloat16), output), scales[0:1])
    hidden = jnp.maximum(dot(middle.astype(jnp.bfloat16), expand), 0.0).astype(jnp.bfloat16)
    return layer_norm(middle + dot(hidden, shrink), scales[1:2])


def update_frames(states, frames, frame_weight):
    update = contract(frame_weight, states, 0, 1, precision=HIGHEST)
    x, y, z = update[0:1], update[1:2], update[2:3]
    length = jnp.sqrt(1.0 + x * x + y * y + z * z)
    w, x, y, z = 1.0 / length, x / length, y / length, z / length
    turn = (
        (w * w + x * x - y * y - z * z, 2.0 * (x * y - w * z), 2.0 * (x * z + w * y)),
        (2.0 * (x * y + w * z), w * w - x * x + y * y - z * z, 2.0 * (y * z - w * x)),
        (2.0 * (x * z - w * y), 2.0 * (y * z + w * x), w * w - x * x - y * y + z * z),
    )
    old = [frames[k : k + 1] for k in range(12)]
    rotation = [
        sum(old[3 * c + d] * turn[d][e] for d in range(3)) for c in range(3) for e in range(3)
    ]
    offset = [
        sum(old[3 * c + d] * update[3 + d : 4 + d] for d in range(3)) + old[9 + c]
        for c in range(3)
    ]
    return jnp.concatenate(rotation + offset, axis=0)


def finish_kernel(
    n_ka,
    hidden_ref,
    pair_ref,
    states_ref,
    mask,
    frames,
    project,
    output,
    expand,
    shrink,
    scales,
    frame_weight,
    to_edge,
    second,
    third,
    biases,
    edge_scale,
    node_out,
    frames_out,
    edges_out,
    row_part,
    key_part,
    live_row,
    live_key,
    states_s,
    key_value,
):
    step, keys, width = pair_ref.shape
    rows = node_out.shape[0]
    count = states_ref.shape[0]
    turn = pl.program_id(0)

    @pl.when(turn == 0)
    def _():
        row_first = pl.multiple_of(lax.axis_index("pb") * rows, rows)
        key_first = pl.multiple_of(lax.axis_index("ka") * keys, keys)
        fill = jnp.where(mask[...] == 1, 0.0, NEG_FILL)
        live = (mask[...] == 1).astype(jnp.bfloat16)
        live = jnp.broadcast_to(live, (16, count))
        at_row = (iota((rows, count), 1) == row_first + iota((rows, count), 0)).astype(jnp.bfloat16)
        at_key = (iota((keys, count), 1) == key_first + iota((keys, count), 0)).astype(jnp.bfloat16)
        live_row[...] = jnp.broadcast_to(contract(at_row, live, 1, 1)[:, 0:1], live_row.shape)
        live_key[...] = jnp.broadcast_to(contract(at_key, live, 1, 1)[:, 0:1], live_key.shape)

        def apply(states, layer):
            return encoder_rows(
                states,
                key_value[...],
                fill,
                project[layer],
                output[layer],
                expand[layer],
                shrink[layer],
                scales[layer],
            )

        key_value[...] = dot(states_ref[...], project[0][:, C_S:]).astype(jnp.bfloat16)
        chunk = math.gcd(count, 256)
        for start in range(0, count, chunk):
            window = slice(start, start + chunk)
            states_s[window, :] = apply(states_ref[window, :].astype(jnp.float32), 0)
        key_value[...] = dot(states_s[...].astype(jnp.bfloat16), project[1][:, C_S:]).astype(
            jnp.bfloat16
        )
        both = jnp.concatenate(
            [states_s[pl.ds(row_first, rows), :], states_s[pl.ds(key_first, keys), :]], axis=0
        )
        final = apply(both, 1)
        node_out[...] = final[:rows]
        row_part[...] = dot(final[:rows].astype(jnp.bfloat16), to_edge[:, :EH])
        key_part[...] = dot(final[rows:].astype(jnp.bfloat16), to_edge[:, EH:]) + biases[0:1]
        frames_out[...] = update_frames(final[:rows], frames[...], frame_weight[...])

    window = pl.ds(pl.multiple_of(turn * step, step), step)
    pair = pair_ref[...].reshape(step * keys, width)
    hidden = hidden_ref[...].astype(jnp.float32)
    hidden = hidden + row_part[window, :][:, None, :] + key_part[...][None]
    hidden = jnp.maximum(hidden, 0.0).astype(jnp.bfloat16).reshape(step * keys, -1)
    middle = dot(hidden, second[...]) + biases[1:2]
    middle = jnp.maximum(middle, 0.0).astype(jnp.bfloat16)
    result = pair.astype(jnp.float32) + dot(middle, third[...])
    normed = layer_norm(result, edge_scale[...]).reshape(step, keys, width)
    live = live_row[window, :][:, None, :] * live_key[...][None]
    edges_out[...] = (normed * live).astype(edges_out.dtype)


def finish(n_ka, hidden, pair, states, *rest):
    rows, keys, width = pair.shape
    frames = rest[1]
    step = 8
    count = states.shape[0]

    def whole(array):
        return pl.BlockSpec(
            array.shape, lambda i: (0,) * len(array.shape), pipeline_mode=pl.Buffered(1)
        )

    outs = (
        jax.ShapeDtypeStruct((rows, C_S), jnp.float32),
        jax.ShapeDtypeStruct(frames.shape, jnp.float32),
        jax.ShapeDtypeStruct(pair.shape, jnp.bfloat16),
    )
    return pl.pallas_call(
        functools.partial(finish_kernel, n_ka),
        grid=(rows // step,),
        out_shape=outs,
        in_specs=[
            pl.BlockSpec((step, keys, EH), lambda i: (i, 0, 0)),
            pl.BlockSpec((step, keys, width), lambda i: (i, 0, 0)),
        ]
        + [whole(array) for array in (states, *rest)],
        out_specs=(
            pl.BlockSpec((rows, C_S), lambda i: (0, 0)),
            pl.BlockSpec(frames.shape, lambda i: (0, 0)),
            pl.BlockSpec((step, keys, width), lambda i: (i, 0, 0)),
        ),
        scratch_shapes=[
            pltpu.VMEM((rows, EH), jnp.float32),
            pltpu.VMEM((keys, EH), jnp.float32),
            pltpu.VMEM((rows, width), jnp.float32),
            pltpu.VMEM((keys, width), jnp.float32),
            pltpu.VMEM((count, C_S), jnp.float32),
            pltpu.VMEM((count, 2 * C_S), jnp.bfloat16),
        ],
        compiler_params=pltpu.CompilerParams(vmem_limit_bytes=40 << 20),
    )(hidden, pair, states, *rest)


def on_device(
    node_states,
    frames,
    edge_states,
    chain_number,
    residue_index,
    padding_mask,
    query_weight,
    key_weight,
    value_weight,
    point_query,
    point_key,
    point_value,
    bias_weight,
    point_gamma,
    relpos_table,
    output_weight,
    attention_scales,
    layer_project,
    layer_output,
    layer_expand,
    layer_shrink,
    layer_scales,
    frame_weight,
    node_to_edge,
    edge_first,
    edge_second,
    edge_third,
    edge_biases,
    edge_scales,
):
    n_pb, n_ka = lax.axis_size("pb"), lax.axis_size("ka")
    mask = padding_mask[None]
    perm_qk, perm_v = by_component(QKP), by_component(VP)
    states, pair, hidden = attend(
        n_pb,
        n_ka,
        (
            node_states,
            frames,
            chain_number[None],
            residue_index[None],
            mask,
            point_query,
            point_key,
            point_value,
            bias_weight,
            point_gamma[None],
            relpos_table,
            attention_scales[None],
            jnp.asarray(perm_qk, jnp.bfloat16),
            jnp.asarray(perm_v, jnp.bfloat16),
            jnp.asarray(perm_v.T, jnp.bfloat16),
            edge_first,
        ),
        (edge_states, query_weight, key_weight, value_weight, output_weight),
    )
    return finish(
        n_ka,
        hidden,
        pair,
        states.reshape(-1, C_S),
        mask,
        frames,
        layer_project,
        layer_output,
        layer_expand,
        layer_shrink,
        layer_scales,
        frame_weight,
        node_to_edge,
        edge_second,
        edge_third,
        edge_biases,
        edge_scales[None],
    )


def solution(mesh):
    placed = [P()] * 29
    placed[:3] = [P("pb", None), P(None, "pb"), P("pb", "ka", None)]
    return jax.shard_map(
        on_device,
        mesh=mesh,
        in_specs=tuple(placed),
        out_specs=(P("pb", None), P(None, "pb"), P("pb", "ka", None)),
        check_vma=False,
    )
```

```python
import functools
import math

import jax
import jax.numpy as jnp
import numpy as np
from jax import lax
from jax.experimental import pallas as pl
from jax.experimental.pallas import tpu as pltpu
from jax.sharding import PartitionSpec as P

C_S = 256
C_Z = 128
HEADS = 8
HD = 256
QKP = 8
VP = 12
EH = 384
RELBINS = 128
LAYERS = 2
TF_HD = 64
LANES = 128

HIGHEST = lax.Precision.HIGHEST
NEG_FILL = -1000000000.0
CHAIN_STEP = 65536.0
LOADS = 20
MESH = pl.DeviceIdType.MESH
VMEM = pl.BlockSpec(memory_space=pltpu.VMEM)
HBM = pl.BlockSpec(memory_space=pltpu.HBM)


def dot(a, b, **options):
    return jnp.dot(a, b, preferred_element_type=jnp.float32, **options)


def contract(a, b, a_dim, b_dim, **options):
    return lax.dot_general(
        a, b, (((a_dim,), (b_dim,)), ((), ())), preferred_element_type=jnp.float32, **options
    )


def iota(shape, dim):
    return lax.broadcasted_iota(jnp.int32, shape, dim)


def layer_norm(values, scales):
    centered = values - jnp.mean(values, axis=-1, keepdims=True)
    variance = jnp.mean(centered * centered, axis=-1, keepdims=True)
    return centered * lax.rsqrt(variance + 1e-05) * scales


def by_component(count):
    target = np.arange(3 * LANES)
    comp, rest = target // LANES, target % LANES
    source = (rest // count * 3 + comp) * count + rest % count
    source = np.where(rest < HEADS * count, source, -1)
    return np.arange(HEADS * 3 * count)[:, None] == source[None, :]


def frame_columns(frames):
    count = frames.shape[0]
    eye = (iota((count, LANES), 0) == iota((count, LANES), 1)).astype(jnp.float32)
    return contract(frames, eye, 0, 0, precision=HIGHEST)


def place(local, columns):
    parts = [local[:, LANES * d : LANES * (d + 1)] for d in range(3)]
    return jnp.concatenate(
        [
            sum(columns[:, 3 * c + d : 3 * c + d + 1] * parts[d] for d in range(3))
            + columns[:, 9 + c : 10 + c]
            for c in range(3)
        ],
        axis=1,
    )


def head_of_lane(count):
    lane = iota((HEADS, 3 * LANES), 1) % LANES
    return (lane // count == iota((HEADS, 3 * LANES), 0)).astype(jnp.float32)


def attend_kernel(
    n_pb,
    n_ka,
    *refs,
):
    sources, refs = refs[:LOADS], refs[LOADS:]
    (states_out, pair_s, hidden_s), refs = refs[:3], refs[3:]
    targets, refs = refs[:LOADS], refs[LOADS:]
    (
        node,
        frames,
        chain,
        index,
        mask,
        relpos,
        edge_s,
        bias_rows_s,
        first,
        wq,
        point_query,
        point_key,
        point_value,
        perm_qk,
        perm_v,
        gamma,
        wk,
        wv,
        scales,
        ow,
    ) = targets
    (
        x_send,
        x_keys,
        f_keys,
        bias_s,
        work_s,
        stats_send,
        stats_recv,
        part_send,
        part_recv,
        columns_s,
        node_s,
        mine,
        load_sem,
            x_send_sem,
        x_recv_sem,
        f_send_sem,
        f_recv_sem,
        s_send_sem,
        s_recv_sem,
        p_send_sem,
        p_recv_sem,
        g_send_sem,
        g_recv_sem,
        h_send_sem,
        h_recv_sem,
    ) = refs
    rows, keys, channels = edge_s.shape
    count = chain.shape[1]
    part = rows // n_ka
    per = n_pb // n_ka
    row, col = lax.axis_index("pb"), lax.axis_index("ka")
    along_pb = [{"pb": lax.rem(row + d, n_pb)} for d in range(1, n_pb)]
    others = [lax.rem(col + d, n_ka) for d in range(1, n_ka)]
    along_ka = [{"ka": other} for other in others]

    barrier = pltpu.get_barrier_semaphore()
    for peer in along_pb + along_ka:
        pl.semaphore_signal(barrier, inc=1, device_id=peer, device_id_type=MESH)
    loads = [
        pltpu.make_async_copy(source, target, load_sem.at[k])
        for k, (source, target) in enumerate(zip(sources, targets))
    ]
    for load in loads:
        load.start()
    for load in loads[:6]:
        load.wait()

    x_send[...] = node[...].astype(jnp.bfloat16)

    code = chain[...].astype(jnp.float32) * CHAIN_STEP + index[...].astype(jnp.float32)
    code = jnp.broadcast_to(code, (8, count))
    at_row = iota((count, LANES), 0) == row * rows + iota((count, LANES), 1)
    row_code = dot(code, at_row.astype(jnp.float32), precision=HIGHEST)[0:1]
    at_key = iota((keys, count), 1) == col * keys + iota((keys, count), 0)
    key_code = contract(at_key.astype(jnp.float32), code, 1, 1, precision=HIGHEST)[:, 0:1]
    reach = (RELBINS - 2) // 2
    gap = row_code - key_code
    bins = jnp.where(
        jnp.abs(gap) < CHAIN_STEP / 2, jnp.clip(gap, -reach, reach) + reach, RELBINS - 1.0
    )
    table = relpos[...]
    high = table.astype(jnp.bfloat16)
    low = (table - high.astype(jnp.float32)).astype(jnp.bfloat16)
    table = jnp.concatenate([high, low], axis=1)
    bin_lane = iota((keys, RELBINS), 1).astype(jnp.float32)
    for load in loads[6:8]:
        load.wait()
    bias_rows = bias_rows_s[...]

    def pair_rows(start, size):
        onehot = jnp.concatenate(
            [
                jnp.where(bins[:, i : i + 1] == bin_lane, 1.0, 0.0).astype(jnp.bfloat16)
                for i in range(start, start + size)
            ],
            axis=0,
        )
        relative = dot(onehot, table)
        relative = relative[:, :channels] + relative[:, channels:]
        values = edge_s[start : start + size].astype(jnp.float32).reshape(size * keys, channels)
        values = (values + relative).astype(jnp.bfloat16)
        pair_s[start : start + size] = values.reshape(size, keys, channels)
        for i in range(size):
            bias_s[(start + i) * HEADS : (start + i + 1) * HEADS, :] = contract(
                bias_rows, values[i * keys : (i + 1) * keys], 1, 1
            )

    group = 8
    starts = list(range(0, rows, group))
    early = starts[: len(starts) // 2]
    late = starts[len(starts) // 2 :]
    for start in early:
        pair_rows(start, group)

    pl.semaphore_wait(barrier, len(along_pb) + len(along_ka))
    for slot in range(per):

        @pl.when(row == col * per + slot)
        def _():
            copies = []
            for d, peer in enumerate(along_pb):
                copies.append(
                    pltpu.make_async_remote_copy(
                        src_ref=x_send,
                        dst_ref=x_keys.at[slot],
                        send_sem=x_send_sem.at[d],
                        recv_sem=x_recv_sem.at[slot],
                        device_id=peer,
                        device_id_type=MESH,
                    )
                )
                copies.append(
                    pltpu.make_async_remote_copy(
                        src_ref=frames,
                        dst_ref=f_keys.at[slot],
                        send_sem=f_send_sem.at[d],
                        recv_sem=f_recv_sem.at[slot],
                        device_id=peer,
                        device_id_type=MESH,
                    )
                )
            for copy in copies:
                copy.start()
            x_keys[slot] = x_send[...]
            f_keys[slot] = frames[...]

    for start in late:
        pair_rows(start, group)

    own_columns = frame_columns(frames[...])
    for a in range(n_ka):
        columns_s[a] = own_columns[a * part : (a + 1) * part]
        node_s[a] = node[a * part : (a + 1) * part, :]
    own = x_send[...]
    for load in loads[8:16]:
        load.wait()
    queries = dot(own, wq[...]).astype(jnp.bfloat16)
    spread = dot(perm_qk[...], point_query[...]).astype(jnp.bfloat16)
    query_places = place(contract(own, spread, 1, 1), own_columns)
    spread_key = dot(perm_qk[...], point_key[...]).astype(jnp.bfloat16)
    spread_value = dot(perm_v[...], point_value[...]).astype(jnp.bfloat16)
    heads_qk = head_of_lane(QKP)
    by_head = (query_places[:, None, :] * heads_qk[None]).reshape(rows * HEADS, 3 * LANES)
    query_square = jnp.sum(by_head * by_head, axis=-1, keepdims=True)

    for slot in range(per):

        @pl.when(row != col * per + slot)
        def _():
            pltpu.make_async_remote_copy(
                src_ref=x_send,
                dst_ref=x_keys.at[slot],
                send_sem=x_send_sem.at[0],
                recv_sem=x_recv_sem.at[slot],
                device_id=along_pb[0],
                device_id_type=MESH,
            ).wait_recv()
            pltpu.make_async_remote_copy(
                src_ref=frames,
                dst_ref=f_keys.at[slot],
                send_sem=f_send_sem.at[0],
                recv_sem=f_recv_sem.at[slot],
                device_id=along_pb[0],
                device_id_type=MESH,
            ).wait_recv()

    key_rows = jnp.concatenate([x_keys[slot] for slot in range(per)], axis=0)
    key_columns = jnp.concatenate([frame_columns(f_keys[slot]) for slot in range(per)], axis=0)
    key_places = place(contract(key_rows, spread_key, 1, 1), key_columns)
    cross = contract(by_head, key_places, 1, 1, precision=HIGHEST)
    key_square = contract(heads_qk, key_places * key_places, 1, 1, precision=HIGHEST)
    loads[16].wait()
    key_vectors = dot(key_rows, wk[...]).astype(jnp.bfloat16)
    for head in range(HEADS):
        window = slice(head * HD, (head + 1) * HD)
        work_s[pl.ds(head, rows, stride=HEADS), :] = contract(
            queries[:, window], key_vectors[:, window], 1, 1
        )
    own_head = iota((HEADS, HEADS), 0) == iota((HEADS, HEADS), 1)
    gammas = jnp.sum(jnp.where(own_head, gamma[...], 0.0), axis=1, keepdims=True)
    gammas = gammas * math.sqrt(2.0 / (9.0 * QKP))
    distance = (cross - 0.5 * query_square).reshape(rows, HEADS, keys) - 0.5 * key_square[None]
    logits = math.sqrt(1.0 / 3.0) * (
        work_s[...].reshape(rows, HEADS, keys) * (1.0 / math.sqrt(HD))
        + bias_s[...].reshape(rows, HEADS, keys)
        + gammas[None] * distance
    )
    key_first = pl.multiple_of(col * keys, keys)
    valid = (mask[0:1, pl.ds(key_first, keys)] == 1)[None]
    masked = jnp.where(valid, logits, NEG_FILL)
    top = jnp.max(masked, axis=-1, keepdims=True)
    weights = jnp.where(valid, jnp.exp(masked - top), 0.0)
    total = jnp.sum(weights, axis=-1, keepdims=True)
    lanes = stats_send.shape[-1]
    at_lane = iota((rows, 1, lanes), 0) == iota((rows, 1, lanes), 2)
    stats_send[0] = jnp.sum(jnp.where(at_lane, top, 0.0), axis=0)
    stats_send[1] = jnp.sum(jnp.where(at_lane, total, 0.0), axis=0)
    stats = [
        pltpu.make_async_remote_copy(
            src_ref=stats_send,
            dst_ref=stats_recv.at[d],
            send_sem=s_send_sem.at[d],
            recv_sem=s_recv_sem.at[d],
            device_id=peer,
            device_id_type=MESH,
        )
        for d, peer in enumerate(along_ka)
    ]
    for copy in stats:
        copy.start()

    work_s[...] = weights.reshape(rows * HEADS, keys)
    rounded = weights.astype(jnp.bfloat16)
    loads[17].wait()
    value_vectors = dot(key_rows, wv[...]).astype(jnp.bfloat16)
    scalar = [
        dot(
            work_s[pl.ds(head, rows, stride=HEADS), :].astype(jnp.bfloat16),
            value_vectors[:, head * HD : (head + 1) * HD],
        )
        for head in range(HEADS)
    ]
    pair_out = jnp.stack([dot(rounded[i], pair_s[i]) for i in range(rows)], axis=0)
    value_places = place(contract(key_rows, spread_value, 1, 1), key_columns)
    heads_v = head_of_lane(VP)
    points = dot(weights.reshape(rows * HEADS, keys), value_places, precision=HIGHEST)

    for copy in stats:
        copy.wait()
    highest = stats_send[0]
    for d in range(n_ka - 1):
        highest = jnp.maximum(highest, stats_recv[d, 0])
    share = jnp.exp(stats_send[0] - highest)
    whole = stats_send[1] * share
    for d in range(n_ka - 1):
        whole = whole + stats_recv[d, 1] * jnp.exp(stats_recv[d, 0] - highest)
    real_row = iota(whole.shape, 1) < rows
    share = jnp.where(real_row, share / jnp.where(real_row, whole, 1.0), 0.0)
    factor = jnp.sum(jnp.where(at_lane, share[None], 0.0), axis=-1, keepdims=True)
    bias_s[...] = jnp.broadcast_to(factor, (rows, HEADS, keys)).reshape(rows * HEADS, keys)
    work_s[...] = (pair_out * factor).reshape(rows * HEADS, channels)
    for load in loads[18:]:
        load.wait()
    features = []
    for head in range(HEADS):
        scale = bias_s[pl.ds(head, rows, stride=HEADS), :]
        for half in range(HD // LANES):
            features.append(scalar[head][:, half * LANES : (half + 1) * LANES] * scale)
    for head in range(HEADS):
        features.append(work_s[pl.ds(head, rows, stride=HEADS), :])
    features = jnp.concatenate([piece.astype(jnp.bfloat16) for piece in features], axis=1)
    partial = dot(features, ow[: features.shape[1], :])
    points = points.reshape(rows, HEADS, 3 * LANES) * (heads_v[None] * factor)
    points = jnp.sum(points, axis=1)
    partial = jnp.concatenate([partial, points], axis=1)
    for a in range(n_ka):
        part_send[a] = partial[a * part : (a + 1) * part].astype(jnp.bfloat16)
    parts = [
        pltpu.make_async_remote_copy(
            src_ref=part_send.at[other],
            dst_ref=part_recv.at[d],
            send_sem=p_send_sem.at[d],
            recv_sem=p_recv_sem.at[d],
            device_id={"ka": other},
            device_id_type=MESH,
        )
        for d, other in enumerate(others)
    ]
    for copy in parts:
        copy.start()

    def hidden_rows(start):
        pair = pair_s[start : start + group].reshape(group * keys, channels)
        values = dot(pair, first[...]).astype(jnp.bfloat16)
        hidden_s[start : start + group] = values.reshape(group, keys, EH)

    third = -(-len(starts) // 3)
    for start in starts[:third]:
        hidden_rows(start)
    value_base = HEADS * (HD + C_Z)
    point_weight = dot(perm_v[...], ow[value_base : value_base + HEADS * 3 * VP, :]).astype(
        jnp.bfloat16
    )
    for copy in parts:
        copy.wait()
    merged = part_send[col].astype(jnp.float32)
    for d in range(n_ka - 1):
        merged = merged + part_recv[d].astype(jnp.float32)
    columns = columns_s[col]
    moved = [
        merged[:, C_S + LANES * c : C_S + LANES * (c + 1)] - columns[:, 9 + c : 10 + c]
        for c in range(3)
    ]
    local = [
        sum(columns[:, 3 * c + d : 3 * c + d + 1] * moved[c] for c in range(3)) for d in range(3)
    ]
    lengths = jnp.sqrt(sum(piece * piece for piece in local) + 1e-08)
    local = jnp.concatenate([piece.astype(jnp.bfloat16) for piece in local], axis=1)
    length_weight = ow[value_base + HEADS * 3 * VP :, :]
    states = (
        node_s[col]
        + merged[:, :C_S]
        + dot(local, point_weight)
        + dot(lengths[:, : HEADS * VP].astype(jnp.bfloat16), length_weight)
    )
    mine[...] = layer_norm(states, scales[...]).astype(jnp.bfloat16)
    states_out[row, col] = mine[...]
    gathers = [
        pltpu.make_async_remote_copy(
            src_ref=mine,
            dst_ref=states_out.at[row, col],
            send_sem=g_send_sem.at[d],
            recv_sem=g_recv_sem.at[d],
            device_id=peer,
            device_id_type=MESH,
        )
        for d, peer in enumerate(along_pb)
    ]
    for copy in gathers:
        copy.start()
    for start in starts[third : 2 * third]:
        hidden_rows(start)
    for copy in gathers:
        copy.wait()
    spreads = [
        pltpu.make_async_remote_copy(
            src_ref=states_out.at[:, col],
            dst_ref=states_out.at[:, col],
            send_sem=h_send_sem.at[d],
            recv_sem=h_recv_sem.at[d],
            device_id=peer,
            device_id_type=MESH,
        )
        for d, peer in enumerate(along_ka)
    ]
    for copy in spreads:
        copy.start()
    for start in starts[2 * third :]:
        hidden_rows(start)
    for slot in range(per):

        @pl.when(row == col * per + slot)
        def _():
            for d, peer in enumerate(along_pb):
                pltpu.make_async_remote_copy(
                    src_ref=x_send,
                    dst_ref=x_keys.at[slot],
                    send_sem=x_send_sem.at[d],
                    recv_sem=x_recv_sem.at[slot],
                    device_id=peer,
                    device_id_type=MESH,
                ).wait_send()
                pltpu.make_async_remote_copy(
                    src_ref=frames,
                    dst_ref=f_keys.at[slot],
                    send_sem=f_send_sem.at[d],
                    recv_sem=f_recv_sem.at[slot],
                    device_id=peer,
                    device_id_type=MESH,
                ).wait_send()

    for copy in spreads:
        copy.wait()


def attend(n_pb, n_ka, *operands):
    frames, edge = operands[1], operands[6]
    rows, keys, channels = edge.shape
    part, per = rows // n_ka, n_pb // n_ka
    lanes = -(-rows // LANES) * LANES
    bf16, f32 = jnp.bfloat16, jnp.float32
    dma = pltpu.SemaphoreType.DMA
    return pl.pallas_call(
        functools.partial(attend_kernel, n_pb, n_ka),
        out_shape=(
            jax.ShapeDtypeStruct((n_pb, n_ka, part, C_S), bf16),
            jax.ShapeDtypeStruct(edge.shape, bf16),
            jax.ShapeDtypeStruct((rows, keys, EH), bf16),
        ),
        in_specs=[HBM] * len(operands),
        out_specs=(VMEM,) * 3,
        scratch_shapes=[
            *[pltpu.VMEM(array.shape, array.dtype) for array in operands],
            pltpu.VMEM((rows, C_S), bf16),
            pltpu.VMEM((per, rows, C_S), bf16),
            pltpu.VMEM((per,) + frames.shape, f32),
            pltpu.VMEM((rows * HEADS, keys), f32),
            pltpu.VMEM((rows * HEADS, keys), f32),
            pltpu.VMEM((2, HEADS, lanes), f32),
            pltpu.VMEM((n_ka - 1, 2, HEADS, lanes), f32),
            pltpu.VMEM((n_ka, part, C_S + 3 * LANES), bf16),
            pltpu.VMEM((n_ka - 1, part, C_S + 3 * LANES), bf16),
            pltpu.VMEM((n_ka, part, LANES), f32),
            pltpu.VMEM((n_ka, part, C_S), f32),
            pltpu.VMEM((part, C_S), bf16),
            dma((len(operands),)),
            dma((n_pb - 1,)),
            dma((per,)),
            dma((n_pb - 1,)),
            dma((per,)),
            dma((n_ka - 1,)),
            dma((n_ka - 1,)),
            dma((n_ka - 1,)),
            dma((n_ka - 1,)),
            dma((n_pb - 1,)),
            dma((n_pb - 1,)),
            dma((n_ka - 1,)),
            dma((n_ka - 1,)),
        ],
        compiler_params=pltpu.CompilerParams(
            collective_id=0, has_side_effects=True, vmem_limit_bytes=28 << 20
        ),
    )(*[pltpu.with_memory_space_constraint(array, pltpu.HBM) for array in operands])


def encoder_rows(states, key_value, fill, project, output, expand, shrink, scales):
    queries = dot(states.astype(jnp.bfloat16), project[:, :C_S]).astype(
        jnp.bfloat16
    ) * jnp.asarray(1.0 / math.sqrt(TF_HD), jnp.bfloat16)
    owner = iota((1, C_S), 1) // TF_HD
    context = jnp.zeros(states.shape, jnp.float32)
    for head in range(C_S // TF_HD):
        only = jnp.where(owner == head, 1.0, 0.0)
        scores = contract(queries * only.astype(jnp.bfloat16), key_value[:, :C_S], 1, 1) + fill
        weights = jnp.exp(scores - jnp.max(scores, axis=-1, keepdims=True))
        inverse = 1.0 / jnp.sum(weights, axis=-1, keepdims=True)
        mixed = dot(weights.astype(jnp.bfloat16), key_value[:, C_S:])
        context = context + mixed * (inverse * only)
    middle = layer_norm(states + dot(context.astype(jnp.bfloat16), output), scales[0:1])
    hidden = jnp.maximum(dot(middle.astype(jnp.bfloat16), expand), 0.0).astype(jnp.bfloat16)
    return layer_norm(middle + dot(hidden, shrink), scales[1:2])


def update_frames(states, frames, frame_weight):
    update = contract(frame_weight, states, 1, 1, precision=HIGHEST)
    x, y, z = update[0:1], update[1:2], update[2:3]
    length = jnp.sqrt(1.0 + x * x + y * y + z * z)
    w, x, y, z = 1.0 / length, x / length, y / length, z / length
    turn = (
        (w * w + x * x - y * y - z * z, 2.0 * (x * y - w * z), 2.0 * (x * z + w * y)),
        (2.0 * (x * y + w * z), w * w - x * x + y * y - z * z, 2.0 * (y * z - w * x)),
        (2.0 * (x * z - w * y), 2.0 * (y * z + w * x), w * w - x * x - y * y + z * z),
    )
    old = [frames[k : k + 1] for k in range(12)]
    rotation = [
        sum(old[3 * c + d] * turn[d][e] for d in range(3)) for c in range(3) for e in range(3)
    ]
    offset = [
        sum(old[3 * c + d] * update[3 + d : 4 + d] for d in range(3)) + old[9 + c]
        for c in range(3)
    ]
    return jnp.concatenate(rotation + offset, axis=0)


def finish_kernel(
    n_ka,
    hidden_ref,
    pair_ref,
    states_ref,
    mask,
    frames,
    project,
    output,
    expand,
    shrink,
    scales,
    frame_weight,
    to_edge,
    second,
    third,
    biases,
    edge_scale,
    node_out,
    frames_out,
    edges_out,
    row_part,
    key_part,
    live_row,
    live_key,
    states_s,
    key_value,
):
    step, keys, width = pair_ref.shape
    rows = node_out.shape[0]
    count = states_ref.shape[0]
    turn = pl.program_id(0)

    @pl.when(turn == 0)
    def _():
        row_first = pl.multiple_of(lax.axis_index("pb") * rows, rows)
        key_first = pl.multiple_of(lax.axis_index("ka") * keys, keys)
        fill = jnp.where(mask[...] == 1, 0.0, NEG_FILL)
        live = (mask[...] == 1).astype(jnp.bfloat16)
        live = jnp.broadcast_to(live, (16, count))
        at_row = (iota((rows, count), 1) == row_first + iota((rows, count), 0)).astype(jnp.bfloat16)
        at_key = (iota((keys, count), 1) == key_first + iota((keys, count), 0)).astype(jnp.bfloat16)
        live_row[...] = jnp.broadcast_to(contract(at_row, live, 1, 1)[:, 0:1], live_row.shape)
        live_key[...] = jnp.broadcast_to(contract(at_key, live, 1, 1)[:, 0:1], live_key.shape)

        def apply(states, layer):
            return encoder_rows(
                states,
                key_value[...],
                fill,
                project[layer],
                output[layer],
                expand[layer],
                shrink[layer],
                scales[layer],
            )

        key_value[...] = dot(states_ref[...], project[0][:, C_S:]).astype(jnp.bfloat16)
        chunk = math.gcd(count, 256)
        for start in range(0, count, chunk):
            window = slice(start, start + chunk)
            states_s[window, :] = apply(states_ref[window, :].astype(jnp.float32), 0)
        key_value[...] = dot(states_s[...].astype(jnp.bfloat16), project[1][:, C_S:]).astype(
            jnp.bfloat16
        )
        both = jnp.concatenate(
            [states_s[pl.ds(row_first, rows), :], states_s[pl.ds(key_first, keys), :]], axis=0
        )
        final = apply(both, 1)
        node_out[...] = final[:rows]
        row_part[...] = dot(final[:rows].astype(jnp.bfloat16), to_edge[:, :EH])
        key_part[...] = dot(final[rows:].astype(jnp.bfloat16), to_edge[:, EH:]) + biases[0:1]
        frames_out[...] = update_frames(final[:rows], frames[...], frame_weight[...])

    window = pl.ds(pl.multiple_of(turn * step, step), step)
    pair = pair_ref[...].reshape(step * keys, width)
    hidden = hidden_ref[...].astype(jnp.float32)
    hidden = hidden + row_part[window, :][:, None, :] + key_part[...][None]
    hidden = jnp.maximum(hidden, 0.0).astype(jnp.bfloat16).reshape(step * keys, -1)
    middle = dot(hidden, second[...]) + biases[1:2]
    middle = jnp.maximum(middle, 0.0).astype(jnp.bfloat16)
    result = pair.astype(jnp.float32) + dot(middle, third[...])
    normed = layer_norm(result, edge_scale[...]).reshape(step, keys, width)
    live = live_row[window, :][:, None, :] * live_key[...][None]
    edges_out[...] = (normed * live).astype(edges_out.dtype)


def finish(n_ka, hidden, pair, states, *rest):
    rows, keys, width = pair.shape
    frames = rest[1]
    step = 8
    count = states.shape[0]

    def whole(array):
        return pl.BlockSpec(
            array.shape, lambda i: (0,) * len(array.shape), pipeline_mode=pl.Buffered(1)
        )

    outs = (
        jax.ShapeDtypeStruct((rows, C_S), jnp.float32),
        jax.ShapeDtypeStruct(frames.shape, jnp.float32),
        jax.ShapeDtypeStruct(pair.shape, jnp.bfloat16),
    )
    return pl.pallas_call(
        functools.partial(finish_kernel, n_ka),
        grid=(rows // step,),
        out_shape=outs,
        in_specs=[
            pl.BlockSpec((step, keys, EH), lambda i: (i, 0, 0)),
            pl.BlockSpec((step, keys, width), lambda i: (i, 0, 0)),
        ]
        + [whole(array) for array in (states, *rest)],
        out_specs=(
            pl.BlockSpec((rows, C_S), lambda i: (0, 0)),
            pl.BlockSpec(frames.shape, lambda i: (0, 0)),
            pl.BlockSpec((step, keys, width), lambda i: (i, 0, 0)),
        ),
        scratch_shapes=[
            pltpu.VMEM((rows, EH), jnp.float32),
            pltpu.VMEM((keys, EH), jnp.float32),
            pltpu.VMEM((rows, width), jnp.float32),
            pltpu.VMEM((keys, width), jnp.float32),
            pltpu.VMEM((count, C_S), jnp.float32),
            pltpu.VMEM((count, 2 * C_S), jnp.bfloat16),
        ],
        compiler_params=pltpu.CompilerParams(vmem_limit_bytes=28 << 20),
    )(hidden, pair, states, *rest)


def on_device(
    node_states,
    frames,
    edge_states,
    chain_number,
    residue_index,
    padding_mask,
    query_weight,
    key_weight,
    value_weight,
    point_query,
    point_key,
    point_value,
    bias_weight,
    point_gamma,
    relpos_table,
    output_weight,
    attention_scales,
    layer_project,
    layer_output,
    layer_expand,
    layer_shrink,
    layer_scales,
    frame_weight,
    node_to_edge,
    edge_first,
    edge_second,
    edge_third,
    edge_biases,
    edge_scales,
):
    n_pb, n_ka = lax.axis_size("pb"), lax.axis_size("ka")
    mask = padding_mask[None]
    perm_qk, perm_v = (jnp.asarray(by_component(k).T, jnp.bfloat16) for k in (QKP, VP))
    states, pair, hidden = attend(
        n_pb,
        n_ka,
        node_states,
        frames,
        chain_number[None],
        residue_index[None],
        mask,
        relpos_table,
        edge_states,
        jnp.transpose(bias_weight),
        edge_first,
        query_weight,
        jnp.transpose(point_query),
        jnp.transpose(point_key),
        jnp.transpose(point_value),
        perm_qk,
        perm_v,
        point_gamma[None],
        key_weight,
        value_weight,
        attention_scales[None],
        output_weight,
    )
    return finish(
        n_ka,
        hidden,
        pair,
        states.reshape(-1, C_S),
        mask,
        frames,
        layer_project,
        layer_output,
        layer_expand,
        layer_shrink,
        layer_scales,
        jnp.transpose(frame_weight),
        node_to_edge,
        edge_second,
        edge_third,
        edge_biases,
        edge_scales[None],
    )


def solution(mesh):
    placed = [P()] * 29
    placed[:3] = [P("pb", None), P(None, "pb"), P("pb", "ka", None)]
    return jax.shard_map(
        on_device,
        mesh=mesh,
        in_specs=tuple(placed),
        out_specs=(P("pb", None), P(None, "pb"), P("pb", "ka", None)),
        check_vma=False,
    )
```

```python
import functools
import math

import jax
import jax.numpy as jnp
import numpy as np
from jax import lax
from jax.experimental import pallas as pl
from jax.experimental.pallas import tpu as pltpu
from jax.sharding import PartitionSpec as P

C_S = 256
C_Z = 128
HEADS = 8
HD = 256
QKP = 8
VP = 12
EH = 384
RELBINS = 128
LAYERS = 2
TF_HD = 64
LANES = 128

HIGHEST = lax.Precision.HIGHEST
NEG_FILL = -1000000000.0
CHAIN_STEP = 65536.0
LOADS = 20
MESH = pl.DeviceIdType.MESH
VMEM = pl.BlockSpec(memory_space=pltpu.VMEM)
HBM = pl.BlockSpec(memory_space=pltpu.HBM)


def dot(a, b, **options):
    return jnp.dot(a, b, preferred_element_type=jnp.float32, **options)


def contract(a, b, a_dim, b_dim, **options):
    return lax.dot_general(
        a, b, (((a_dim,), (b_dim,)), ((), ())), preferred_element_type=jnp.float32, **options
    )


def iota(shape, dim):
    return lax.broadcasted_iota(jnp.int32, shape, dim)


def layer_norm(values, scales):
    centered = values - jnp.mean(values, axis=-1, keepdims=True)
    variance = jnp.mean(centered * centered, axis=-1, keepdims=True)
    return centered * lax.rsqrt(variance + 1e-05) * scales


def by_component(count):
    target = np.arange(3 * LANES)
    comp, rest = target // LANES, target % LANES
    source = (rest // count * 3 + comp) * count + rest % count
    source = np.where(rest < HEADS * count, source, -1)
    return np.arange(HEADS * 3 * count)[:, None] == source[None, :]


def frame_columns(frames):
    count = frames.shape[0]
    eye = (iota((count, LANES), 0) == iota((count, LANES), 1)).astype(jnp.float32)
    return contract(frames, eye, 0, 0, precision=HIGHEST)


def place(local, columns):
    parts = [local[:, LANES * d : LANES * (d + 1)] for d in range(3)]
    return jnp.concatenate(
        [
            sum(columns[:, 3 * c + d : 3 * c + d + 1] * parts[d] for d in range(3))
            + columns[:, 9 + c : 10 + c]
            for c in range(3)
        ],
        axis=1,
    )


def head_of_lane(count):
    lane = iota((HEADS, 3 * LANES), 1) % LANES
    return (lane // count == iota((HEADS, 3 * LANES), 0)).astype(jnp.float32)


def attend_kernel(
    n_pb,
    n_ka,
    *refs,
):
    sources, refs = refs[:LOADS], refs[LOADS:]
    (states_out, pair_s, hidden_s), refs = refs[:3], refs[3:]
    targets, refs = refs[:LOADS], refs[LOADS:]
    (
        node,
        frames,
        chain,
        index,
        mask,
        relpos,
        edge_s,
        bias_rows_s,
        first,
        wq,
        point_query,
        point_key,
        point_value,
        perm_qk,
        perm_v,
        gamma,
        wk,
        wv,
        scales,
        ow,
    ) = targets
    (
        x_send,
        f_send,
        x_keys,
        f_keys,
        bias_s,
        work_s,
        stats_send,
        stats_recv,
        part_send,
        part_recv,
        columns_s,
        node_s,
        mine,
        load_sem,
            x_send_sem,
        x_recv_sem,
        f_send_sem,
        f_recv_sem,
        s_send_sem,
        s_recv_sem,
        p_send_sem,
        p_recv_sem,
        g_send_sem,
        g_recv_sem,
        h_send_sem,
        h_recv_sem,
    ) = refs
    rows, keys, channels = edge_s.shape
    count = chain.shape[1]
    part = rows // n_ka
    per = n_pb // n_ka
    row, col = lax.axis_index("pb"), lax.axis_index("ka")
    along_pb = [{"pb": lax.rem(row + d, n_pb)} for d in range(1, n_pb)]
    others = [lax.rem(col + d, n_ka) for d in range(1, n_ka)]
    along_ka = [{"ka": other} for other in others]

    barrier = pltpu.get_barrier_semaphore()
    for peer in along_pb + along_ka:
        pl.semaphore_signal(barrier, inc=1, device_id=peer, device_id_type=MESH)
    loads = [
        pltpu.make_async_copy(source, target, load_sem.at[k])
        for k, (source, target) in enumerate(zip(sources, targets))
    ]
    for load in loads:
        load.start()
    for load in loads[:6]:
        load.wait()

    x_send[...] = node[...].astype(jnp.bfloat16)
    f_send[...] = frames[...].astype(jnp.bfloat16)

    code = chain[...].astype(jnp.float32) * CHAIN_STEP + index[...].astype(jnp.float32)
    code = jnp.broadcast_to(code, (8, count))
    at_row = iota((count, LANES), 0) == row * rows + iota((count, LANES), 1)
    row_code = dot(code, at_row.astype(jnp.float32), precision=HIGHEST)[0:1]
    at_key = iota((keys, count), 1) == col * keys + iota((keys, count), 0)
    key_code = contract(at_key.astype(jnp.float32), code, 1, 1, precision=HIGHEST)[:, 0:1]
    reach = (RELBINS - 2) // 2
    gap = row_code - key_code
    bins = jnp.where(
        jnp.abs(gap) < CHAIN_STEP / 2, jnp.clip(gap, -reach, reach) + reach, RELBINS - 1.0
    )
    table = relpos[...]
    high = table.astype(jnp.bfloat16)
    low = (table - high.astype(jnp.float32)).astype(jnp.bfloat16)
    table = jnp.concatenate([high, low], axis=1)
    bin_lane = iota((keys, RELBINS), 1).astype(jnp.float32)
    for load in loads[6:8]:
        load.wait()
    bias_rows = bias_rows_s[...]

    def pair_rows(start, size):
        onehot = jnp.concatenate(
            [
                jnp.where(bins[:, i : i + 1] == bin_lane, 1.0, 0.0).astype(jnp.bfloat16)
                for i in range(start, start + size)
            ],
            axis=0,
        )
        relative = dot(onehot, table)
        relative = relative[:, :channels] + relative[:, channels:]
        values = edge_s[start : start + size].astype(jnp.float32).reshape(size * keys, channels)
        values = (values + relative).astype(jnp.bfloat16)
        pair_s[start : start + size] = values.reshape(size, keys, channels)
        for i in range(size):
            bias_s[(start + i) * HEADS : (start + i + 1) * HEADS, :] = contract(
                bias_rows, values[i * keys : (i + 1) * keys], 1, 1
            )

    group = 8
    starts = list(range(0, rows, group))
    early = starts[: len(starts) // 4]
    late = starts[len(starts) // 4 :]
    for start in early:
        pair_rows(start, group)

    pl.semaphore_wait(barrier, len(along_pb) + len(along_ka))
    for slot in range(per):

        @pl.when(row == col * per + slot)
        def _():
            copies = []
            for d, peer in enumerate(along_pb):
                copies.append(
                    pltpu.make_async_remote_copy(
                        src_ref=x_send,
                        dst_ref=x_keys.at[slot],
                        send_sem=x_send_sem.at[d],
                        recv_sem=x_recv_sem.at[slot],
                        device_id=peer,
                        device_id_type=MESH,
                    )
                )
                copies.append(
                    pltpu.make_async_remote_copy(
                        src_ref=f_send,
                        dst_ref=f_keys.at[slot],
                        send_sem=f_send_sem.at[d],
                        recv_sem=f_recv_sem.at[slot],
                        device_id=peer,
                        device_id_type=MESH,
                    )
                )
            for copy in copies:
                copy.start()
            x_keys[slot] = x_send[...]
            f_keys[slot] = f_send[...]

    for start in late:
        pair_rows(start, group)

    own_columns = frame_columns(frames[...])
    for a in range(n_ka):
        columns_s[a] = own_columns[a * part : (a + 1) * part]
        node_s[a] = node[a * part : (a + 1) * part, :]
    own = x_send[...]
    for load in loads[8:16]:
        load.wait()
    queries = dot(own, wq[...]).astype(jnp.bfloat16)
    spread = dot(perm_qk[...], point_query[...]).astype(jnp.bfloat16)
    query_places = place(contract(own, spread, 1, 1), own_columns)
    spread_key = dot(perm_qk[...], point_key[...]).astype(jnp.bfloat16)
    spread_value = dot(perm_v[...], point_value[...]).astype(jnp.bfloat16)
    heads_qk = head_of_lane(QKP)
    by_head = (query_places[:, None, :] * heads_qk[None]).reshape(rows * HEADS, 3 * LANES)
    query_square = jnp.sum(by_head * by_head, axis=-1, keepdims=True)

    for slot in range(per):

        @pl.when(row != col * per + slot)
        def _():
            pltpu.make_async_remote_copy(
                src_ref=x_send,
                dst_ref=x_keys.at[slot],
                send_sem=x_send_sem.at[0],
                recv_sem=x_recv_sem.at[slot],
                device_id=along_pb[0],
                device_id_type=MESH,
            ).wait_recv()
            pltpu.make_async_remote_copy(
                src_ref=f_send,
                dst_ref=f_keys.at[slot],
                send_sem=f_send_sem.at[0],
                recv_sem=f_recv_sem.at[slot],
                device_id=along_pb[0],
                device_id_type=MESH,
            ).wait_recv()

    key_rows = jnp.concatenate([x_keys[slot] for slot in range(per)], axis=0)
    key_columns = jnp.concatenate([frame_columns(f_keys[slot].astype(jnp.float32)) for slot in range(per)], axis=0)
    key_places = place(contract(key_rows, spread_key, 1, 1), key_columns)
    cross = contract(by_head, key_places, 1, 1, precision=HIGHEST)
    key_square = contract(heads_qk, key_places * key_places, 1, 1, precision=HIGHEST)
    loads[16].wait()
    key_vectors = dot(key_rows, wk[...]).astype(jnp.bfloat16)
    for head in range(HEADS):
        window = slice(head * HD, (head + 1) * HD)
        work_s[pl.ds(head, rows, stride=HEADS), :] = contract(
            queries[:, window], key_vectors[:, window], 1, 1
        )
    own_head = iota((HEADS, HEADS), 0) == iota((HEADS, HEADS), 1)
    gammas = jnp.sum(jnp.where(own_head, gamma[...], 0.0), axis=1, keepdims=True)
    gammas = gammas * math.sqrt(2.0 / (9.0 * QKP))
    distance = (cross - 0.5 * query_square).reshape(rows, HEADS, keys) - 0.5 * key_square[None]
    logits = math.sqrt(1.0 / 3.0) * (
        work_s[...].reshape(rows, HEADS, keys) * (1.0 / math.sqrt(HD))
        + bias_s[...].reshape(rows, HEADS, keys)
        + gammas[None] * distance
    )
    key_first = pl.multiple_of(col * keys, keys)
    valid = (mask[0:1, pl.ds(key_first, keys)] == 1)[None]
    masked = jnp.where(valid, logits, NEG_FILL)
    top = jnp.max(masked, axis=-1, keepdims=True)
    weights = jnp.where(valid, jnp.exp(masked - top), 0.0)
    total = jnp.sum(weights, axis=-1, keepdims=True)
    lanes = stats_send.shape[-1]
    at_lane = iota((rows, 1, lanes), 0) == iota((rows, 1, lanes), 2)
    stats_send[0] = jnp.sum(jnp.where(at_lane, top, 0.0), axis=0)
    stats_send[1] = jnp.sum(jnp.where(at_lane, total, 0.0), axis=0)
    stats = [
        pltpu.make_async_remote_copy(
            src_ref=stats_send,
            dst_ref=stats_recv.at[d],
            send_sem=s_send_sem.at[d],
            recv_sem=s_recv_sem.at[d],
            device_id=peer,
            device_id_type=MESH,
        )
        for d, peer in enumerate(along_ka)
    ]
    for copy in stats:
        copy.start()

    work_s[...] = weights.reshape(rows * HEADS, keys)
    rounded = weights.astype(jnp.bfloat16)
    loads[17].wait()
    value_vectors = dot(key_rows, wv[...]).astype(jnp.bfloat16)
    scalar = [
        dot(
            work_s[pl.ds(head, rows, stride=HEADS), :].astype(jnp.bfloat16),
            value_vectors[:, head * HD : (head + 1) * HD],
        )
        for head in range(HEADS)
    ]
    pair_out = jnp.stack([dot(rounded[i], pair_s[i]) for i in range(rows)], axis=0)
    value_places = place(contract(key_rows, spread_value, 1, 1), key_columns)
    heads_v = head_of_lane(VP)
    points = dot(weights.reshape(rows * HEADS, keys), value_places, precision=HIGHEST)

    for copy in stats:
        copy.wait()
    highest = stats_send[0]
    for d in range(n_ka - 1):
        highest = jnp.maximum(highest, stats_recv[d, 0])
    share = jnp.exp(stats_send[0] - highest)
    whole = stats_send[1] * share
    for d in range(n_ka - 1):
        whole = whole + stats_recv[d, 1] * jnp.exp(stats_recv[d, 0] - highest)
    real_row = iota(whole.shape, 1) < rows
    share = jnp.where(real_row, share / jnp.where(real_row, whole, 1.0), 0.0)
    factor = jnp.sum(jnp.where(at_lane, share[None], 0.0), axis=-1, keepdims=True)
    bias_s[...] = jnp.broadcast_to(factor, (rows, HEADS, keys)).reshape(rows * HEADS, keys)
    work_s[...] = (pair_out * factor).reshape(rows * HEADS, channels)
    for load in loads[18:]:
        load.wait()
    features = []
    for head in range(HEADS):
        scale = bias_s[pl.ds(head, rows, stride=HEADS), :]
        for half in range(HD // LANES):
            features.append(scalar[head][:, half * LANES : (half + 1) * LANES] * scale)
    for head in range(HEADS):
        features.append(work_s[pl.ds(head, rows, stride=HEADS), :])
    features = jnp.concatenate([piece.astype(jnp.bfloat16) for piece in features], axis=1)
    partial = dot(features, ow[: features.shape[1], :])
    points = points.reshape(rows, HEADS, 3 * LANES) * (heads_v[None] * factor)
    points = jnp.sum(points, axis=1)
    partial = jnp.concatenate([partial, points], axis=1)
    for a in range(n_ka):
        part_send[a] = partial[a * part : (a + 1) * part].astype(jnp.bfloat16)
    parts = [
        pltpu.make_async_remote_copy(
            src_ref=part_send.at[other],
            dst_ref=part_recv.at[d],
            send_sem=p_send_sem.at[d],
            recv_sem=p_recv_sem.at[d],
            device_id={"ka": other},
            device_id_type=MESH,
        )
        for d, other in enumerate(others)
    ]
    for copy in parts:
        copy.start()

    def hidden_rows(start):
        pair = pair_s[start : start + group].reshape(group * keys, channels)
        values = dot(pair, first[...]).astype(jnp.bfloat16)
        hidden_s[start : start + group] = values.reshape(group, keys, EH)

    third = -(-len(starts) // 3)
    for start in starts[:third]:
        hidden_rows(start)
    value_base = HEADS * (HD + C_Z)
    point_weight = dot(perm_v[...], ow[value_base : value_base + HEADS * 3 * VP, :]).astype(
        jnp.bfloat16
    )
    for copy in parts:
        copy.wait()
    merged = part_send[col].astype(jnp.float32)
    for d in range(n_ka - 1):
        merged = merged + part_recv[d].astype(jnp.float32)
    columns = columns_s[col]
    moved = [
        merged[:, C_S + LANES * c : C_S + LANES * (c + 1)] - columns[:, 9 + c : 10 + c]
        for c in range(3)
    ]
    local = [
        sum(columns[:, 3 * c + d : 3 * c + d + 1] * moved[c] for c in range(3)) for d in range(3)
    ]
    lengths = jnp.sqrt(sum(piece * piece for piece in local) + 1e-08)
    local = jnp.concatenate([piece.astype(jnp.bfloat16) for piece in local], axis=1)
    length_weight = ow[value_base + HEADS * 3 * VP :, :]
    states = (
        node_s[col]
        + merged[:, :C_S]
        + dot(local, point_weight)
        + dot(lengths[:, : HEADS * VP].astype(jnp.bfloat16), length_weight)
    )
    mine[...] = layer_norm(states, scales[...]).astype(jnp.bfloat16)
    states_out[row, col] = mine[...]
    gathers = [
        pltpu.make_async_remote_copy(
            src_ref=mine,
            dst_ref=states_out.at[row, col],
            send_sem=g_send_sem.at[d],
            recv_sem=g_recv_sem.at[d],
            device_id=peer,
            device_id_type=MESH,
        )
        for d, peer in enumerate(along_pb)
    ]
    for copy in gathers:
        copy.start()

    def forward(distance):
        source = lax.rem(row + n_pb - distance, n_pb)
        copies = [
            pltpu.make_async_remote_copy(
                src_ref=states_out.at[source, col] if distance else mine,
                dst_ref=states_out.at[source, col],
                send_sem=h_send_sem.at[distance, d],
                recv_sem=h_recv_sem.at[distance, d],
                device_id=peer,
                device_id_type=MESH,
            )
            for d, peer in enumerate(along_ka)
        ]
        for copy in copies:
            copy.start()
        return copies

    spreads = forward(0)
    for start in starts[third:]:
        hidden_rows(start)
    for distance in sorted(range(1, n_pb), key=lambda d: min(d, n_pb - d)):
        gathers[distance - 1].wait_recv()
        spreads += forward(distance)
    for copy in gathers:
        copy.wait_send()
    for slot in range(per):

        @pl.when(row == col * per + slot)
        def _():
            for d, peer in enumerate(along_pb):
                pltpu.make_async_remote_copy(
                    src_ref=x_send,
                    dst_ref=x_keys.at[slot],
                    send_sem=x_send_sem.at[d],
                    recv_sem=x_recv_sem.at[slot],
                    device_id=peer,
                    device_id_type=MESH,
                ).wait_send()
                pltpu.make_async_remote_copy(
                    src_ref=f_send,
                    dst_ref=f_keys.at[slot],
                    send_sem=f_send_sem.at[d],
                    recv_sem=f_recv_sem.at[slot],
                    device_id=peer,
                    device_id_type=MESH,
                ).wait_send()

    for copy in spreads:
        copy.wait()


def attend(n_pb, n_ka, *operands):
    frames, edge = operands[1], operands[6]
    rows, keys, channels = edge.shape
    part, per = rows // n_ka, n_pb // n_ka
    lanes = -(-rows // LANES) * LANES
    bf16, f32 = jnp.bfloat16, jnp.float32
    dma = pltpu.SemaphoreType.DMA
    return pl.pallas_call(
        functools.partial(attend_kernel, n_pb, n_ka),
        out_shape=(
            jax.ShapeDtypeStruct((n_pb, n_ka, part, C_S), bf16),
            jax.ShapeDtypeStruct(edge.shape, bf16),
            jax.ShapeDtypeStruct((rows, keys, EH), bf16),
        ),
        in_specs=[HBM] * len(operands),
        out_specs=(VMEM,) * 3,
        scratch_shapes=[
            *[pltpu.VMEM(array.shape, array.dtype) for array in operands],
            pltpu.VMEM((rows, C_S), bf16),
            pltpu.VMEM(frames.shape, bf16),
            pltpu.VMEM((per, rows, C_S), bf16),
            pltpu.VMEM((per,) + frames.shape, bf16),
            pltpu.VMEM((rows * HEADS, keys), f32),
            pltpu.VMEM((rows * HEADS, keys), f32),
            pltpu.VMEM((2, HEADS, lanes), f32),
            pltpu.VMEM((n_ka - 1, 2, HEADS, lanes), f32),
            pltpu.VMEM((n_ka, part, C_S + 3 * LANES), bf16),
            pltpu.VMEM((n_ka - 1, part, C_S + 3 * LANES), bf16),
            pltpu.VMEM((n_ka, part, LANES), f32),
            pltpu.VMEM((n_ka, part, C_S), f32),
            pltpu.VMEM((part, C_S), bf16),
            dma((len(operands),)),
            dma((n_pb - 1,)),
            dma((per,)),
            dma((n_pb - 1,)),
            dma((per,)),
            dma((n_ka - 1,)),
            dma((n_ka - 1,)),
            dma((n_ka - 1,)),
            dma((n_ka - 1,)),
            dma((n_pb - 1,)),
            dma((n_pb - 1,)),
            dma((n_pb, n_ka - 1)),
            dma((n_pb, n_ka - 1)),
        ],
        compiler_params=pltpu.CompilerParams(
            collective_id=0, has_side_effects=True, vmem_limit_bytes=28 << 20
        ),
    )(*[pltpu.with_memory_space_constraint(array, pltpu.HBM) for array in operands])


def encoder_rows(states, keys, values, fill, project, output, expand, shrink, scales):
    queries = dot(states.astype(jnp.bfloat16), project[:, :C_S]).astype(
        jnp.bfloat16
    ) * jnp.asarray(1.0 / math.sqrt(TF_HD), jnp.bfloat16)
    owner = iota((1, C_S), 1) // TF_HD
    context = []
    for half in range(C_S // LANES):
        mixed = None
        for head in range(half * LANES // TF_HD, (half + 1) * LANES // TF_HD):
            only = jnp.where(owner == head, 1.0, 0.0).astype(jnp.bfloat16)
            scores = contract(queries * only, keys, 1, 1) + fill
            weights = jnp.exp(scores - jnp.max(scores, axis=-1, keepdims=True))
            sums = dot(weights.astype(jnp.bfloat16), values[head])
            totals = sums[:, (1 - half) * LANES : (2 - half) * LANES]
            sums = sums[:, half * LANES : (half + 1) * LANES] / totals
            mine = owner[:, half * LANES : (half + 1) * LANES] == head
            mixed = sums if mixed is None else jnp.where(mine, sums, mixed)
        context.append(mixed.astype(jnp.bfloat16))
    context = jnp.concatenate(context, axis=1)
    middle = layer_norm(states + dot(context, output), scales[0:1])
    hidden = jnp.maximum(dot(middle.astype(jnp.bfloat16), expand), 0.0).astype(jnp.bfloat16)
    return layer_norm(middle + dot(hidden, shrink), scales[1:2])


def update_frames(states, frames, frame_weight):
    update = contract(frame_weight, states, 1, 1, precision=HIGHEST)
    x, y, z = update[0:1], update[1:2], update[2:3]
    length = jnp.sqrt(1.0 + x * x + y * y + z * z)
    w, x, y, z = 1.0 / length, x / length, y / length, z / length
    turn = (
        (w * w + x * x - y * y - z * z, 2.0 * (x * y - w * z), 2.0 * (x * z + w * y)),
        (2.0 * (x * y + w * z), w * w - x * x + y * y - z * z, 2.0 * (y * z - w * x)),
        (2.0 * (x * z - w * y), 2.0 * (y * z + w * x), w * w - x * x - y * y + z * z),
    )
    old = [frames[k : k + 1] for k in range(12)]
    rotation = [
        sum(old[3 * c + d] * turn[d][e] for d in range(3)) for c in range(3) for e in range(3)
    ]
    offset = [
        sum(old[3 * c + d] * update[3 + d : 4 + d] for d in range(3)) + old[9 + c]
        for c in range(3)
    ]
    return jnp.concatenate(rotation + offset, axis=0)


def finish_kernel(
    n_ka,
    hidden_ref,
    pair_ref,
    states_ref,
    mask,
    frames,
    project,
    output,
    expand,
    shrink,
    scales,
    frame_weight,
    to_edge,
    second,
    third,
    biases,
    edge_scale,
    node_out,
    frames_out,
    edges_out,
    row_part,
    key_part,
    live_row,
    live_key,
    states_s,
    enc_keys,
    enc_values,
    second_tail,
    third_tail,
):
    step, keys, width = pair_ref.shape
    rows = node_out.shape[0]
    count = states_ref.shape[0]
    turn = pl.program_id(0)

    @pl.when(turn == 0)
    def _():
        row_first = pl.multiple_of(lax.axis_index("pb") * rows, rows)
        key_first = pl.multiple_of(lax.axis_index("ka") * keys, keys)
        fill = jnp.where(mask[...] == 1, 0.0, NEG_FILL)
        live = (mask[...] == 1).astype(jnp.bfloat16)
        live = jnp.broadcast_to(live, (16, count))
        at_row = (iota((rows, count), 1) == row_first + iota((rows, count), 0)).astype(jnp.bfloat16)
        at_key = (iota((keys, count), 1) == key_first + iota((keys, count), 0)).astype(jnp.bfloat16)
        live_row[...] = jnp.broadcast_to(contract(at_row, live, 1, 1)[:, 0:1], live_row.shape)
        live_key[...] = jnp.broadcast_to(contract(at_key, live, 1, 1)[:, 0:1], live_key.shape)

        def attended(states, layer):
            both = dot(states.astype(jnp.bfloat16), project[layer][:, C_S:]).astype(jnp.bfloat16)
            enc_keys[...] = both[:, :C_S]
            owner = iota((1, C_S), 1) // TF_HD
            for head in range(C_S // TF_HD):
                values = jnp.where(owner == head, both[:, C_S:].astype(jnp.float32), 1.0)
                enc_values[head] = values.astype(jnp.bfloat16)

        def apply(states, layer):
            return encoder_rows(
                states,
                enc_keys[...],
                enc_values,
                fill,
                project[layer],
                output[layer],
                expand[layer],
                shrink[layer],
                scales[layer],
            )

        attended(states_ref[...], 0)
        chunk = math.gcd(count, 512)
        for start in range(0, count, chunk):
            window = slice(start, start + chunk)
            states_s[window, :] = apply(states_ref[window, :].astype(jnp.float32), 0)
        attended(states_s[...], 1)
        both = jnp.concatenate(
            [states_s[pl.ds(row_first, rows), :], states_s[pl.ds(key_first, keys), :]], axis=0
        )
        final = apply(both, 1)
        node_out[...] = final[:rows]
        row_part[...] = dot(final[:rows].astype(jnp.bfloat16), to_edge[:, :EH])
        key_part[...] = dot(final[rows:].astype(jnp.bfloat16), to_edge[:, EH:]) + biases[0:1]
        wide = EH - LANES
        zeros = jnp.zeros((LANES, LANES), jnp.bfloat16)
        for target, block in (
            (second_tail, second[wide:, wide:]),
            (third_tail, third[wide:, :]),
        ):
            target[...] = jnp.concatenate(
                [
                    jnp.concatenate([block, zeros], axis=1),
                    jnp.concatenate([zeros, block], axis=1),
                ],
                axis=0,
            )
        frames_out[...] = update_frames(final[:rows], frames[...], frame_weight[...])

    window = pl.ds(pl.multiple_of(turn * step, step), step)
    pair = pair_ref[...].reshape(step * keys, width)
    hidden = hidden_ref[...].astype(jnp.float32)
    hidden = hidden + row_part[window, :][:, None, :] + key_part[...][None]
    hidden = jnp.maximum(hidden, 0.0).astype(jnp.bfloat16).reshape(step * keys, -1)
    wide = EH - LANES

    def tail(values, weights):
        half = values.shape[0] // 2
        both = jnp.concatenate([values[:half], values[half:]], axis=1)
        both = dot(both, weights)
        return jnp.concatenate([both[:, :LANES], both[:, LANES:]], axis=0)

    middle = dot(hidden, second[:, :wide]) + biases[1:2, :wide]
    middle = jnp.maximum(middle, 0.0).astype(jnp.bfloat16)
    rest = dot(hidden[:, :wide], second[:wide, wide:]) + tail(hidden[:, wide:], second_tail[...])
    rest = jnp.maximum(rest + biases[1:2, wide:], 0.0).astype(jnp.bfloat16)
    result = pair.astype(jnp.float32) + dot(middle, third[:wide, :]) + tail(rest, third_tail[...])
    normed = layer_norm(result, edge_scale[...]).reshape(step, keys, width)
    live = live_row[window, :][:, None, :] * live_key[...][None]
    edges_out[...] = (normed * live).astype(edges_out.dtype)


def finish(n_ka, hidden, pair, states, *rest):
    rows, keys, width = pair.shape
    frames = rest[1]
    step = math.gcd(rows, 16)
    count = states.shape[0]

    def whole(array):
        return pl.BlockSpec(
            array.shape, lambda i: (0,) * len(array.shape), pipeline_mode=pl.Buffered(1)
        )

    outs = (
        jax.ShapeDtypeStruct((rows, C_S), jnp.float32),
        jax.ShapeDtypeStruct(frames.shape, jnp.float32),
        jax.ShapeDtypeStruct(pair.shape, jnp.bfloat16),
    )
    return pl.pallas_call(
        functools.partial(finish_kernel, n_ka),
        grid=(rows // step,),
        out_shape=outs,
        in_specs=[
            pl.BlockSpec((step, keys, EH), lambda i: (i, 0, 0)),
            pl.BlockSpec((step, keys, width), lambda i: (i, 0, 0)),
        ]
        + [whole(array) for array in (states, *rest)],
        out_specs=(
            pl.BlockSpec((rows, C_S), lambda i: (0, 0)),
            pl.BlockSpec(frames.shape, lambda i: (0, 0)),
            pl.BlockSpec((step, keys, width), lambda i: (i, 0, 0)),
        ),
        scratch_shapes=[
            pltpu.VMEM((rows, EH), jnp.float32),
            pltpu.VMEM((keys, EH), jnp.float32),
            pltpu.VMEM((rows, width), jnp.float32),
            pltpu.VMEM((keys, width), jnp.float32),
            pltpu.VMEM((count, C_S), jnp.float32),
            pltpu.VMEM((count, C_S), jnp.bfloat16),
            pltpu.VMEM((C_S // TF_HD, count, C_S), jnp.bfloat16),
            pltpu.VMEM((2 * LANES, 2 * LANES), jnp.bfloat16),
            pltpu.VMEM((2 * LANES, 2 * LANES), jnp.bfloat16),
        ],
        compiler_params=pltpu.CompilerParams(vmem_limit_bytes=28 << 20),
    )(hidden, pair, states, *rest)


def on_device(
    node_states,
    frames,
    edge_states,
    chain_number,
    residue_index,
    padding_mask,
    query_weight,
    key_weight,
    value_weight,
    point_query,
    point_key,
    point_value,
    bias_weight,
    point_gamma,
    relpos_table,
    output_weight,
    attention_scales,
    layer_project,
    layer_output,
    layer_expand,
    layer_shrink,
    layer_scales,
    frame_weight,
    node_to_edge,
    edge_first,
    edge_second,
    edge_third,
    edge_biases,
    edge_scales,
):
    n_pb, n_ka = lax.axis_size("pb"), lax.axis_size("ka")
    mask = padding_mask[None]
    perm_qk, perm_v = (jnp.asarray(by_component(k).T, jnp.bfloat16) for k in (QKP, VP))
    states, pair, hidden = attend(
        n_pb,
        n_ka,
        node_states,
        frames,
        chain_number[None],
        residue_index[None],
        mask,
        relpos_table,
        edge_states,
        jnp.transpose(bias_weight),
        edge_first,
        query_weight,
        jnp.transpose(point_query),
        jnp.transpose(point_key),
        jnp.transpose(point_value),
        perm_qk,
        perm_v,
        point_gamma[None],
        key_weight,
        value_weight,
        attention_scales[None],
        output_weight,
    )
    return finish(
        n_ka,
        hidden,
        pair,
        states.reshape(-1, C_S),
        mask,
        frames,
        layer_project,
        layer_output,
        layer_expand,
        layer_shrink,
        layer_scales,
        jnp.transpose(frame_weight),
        node_to_edge,
        edge_second,
        edge_third,
        edge_biases,
        edge_scales[None],
    )


def solution(mesh):
    placed = [P()] * 29
    placed[:3] = [P("pb", None), P(None, "pb"), P("pb", "ka", None)]
    return jax.shard_map(
        on_device,
        mesh=mesh,
        in_specs=tuple(placed),
        out_specs=(P("pb", None), P(None, "pb"), P("pb", "ka", None)),
        check_vma=False,
    )
```

```python
import functools
import math

import jax
import jax.numpy as jnp
import numpy as np
from jax import lax
from jax.experimental import pallas as pl
from jax.experimental.pallas import tpu as pltpu
from jax.sharding import PartitionSpec as P

C_S = 256
C_Z = 128
HEADS = 8
HD = 256
QKP = 8
VP = 12
EH = 384
RELBINS = 128
LAYERS = 2
TF_HD = 64
LANES = 128

HIGHEST = lax.Precision.HIGHEST
NEG_FILL = -1000000000.0
CHAIN_STEP = 65536.0
LOADS = 20
MESH = pl.DeviceIdType.MESH
VMEM = pl.BlockSpec(memory_space=pltpu.VMEM)
HBM = pl.BlockSpec(memory_space=pltpu.HBM)


def dot(a, b, **options):
    return jnp.dot(a, b, preferred_element_type=jnp.float32, **options)


def contract(a, b, a_dim, b_dim, **options):
    return lax.dot_general(
        a, b, (((a_dim,), (b_dim,)), ((), ())), preferred_element_type=jnp.float32, **options
    )


def iota(shape, dim):
    return lax.broadcasted_iota(jnp.int32, shape, dim)


def layer_norm(values, scales):
    centered = values - jnp.mean(values, axis=-1, keepdims=True)
    variance = jnp.mean(centered * centered, axis=-1, keepdims=True)
    return centered * lax.rsqrt(variance + 1e-05) * scales


def by_component(count):
    target = np.arange(3 * LANES)
    comp, rest = target // LANES, target % LANES
    if LANES % (HEADS * count) == 0:
        rest = rest % (HEADS * count)
    source = (rest // count * 3 + comp) * count + rest % count
    source = np.where(rest < HEADS * count, source, -1)
    return np.arange(HEADS * 3 * count)[:, None] == source[None, :]


def frame_columns(frames):
    count = frames.shape[0]
    eye = (iota((count, LANES), 0) == iota((count, LANES), 1)).astype(jnp.float32)
    return contract(frames, eye, 0, 0, precision=HIGHEST)


def place(local, columns):
    parts = [local[:, LANES * d : LANES * (d + 1)] for d in range(3)]
    return jnp.concatenate(
        [
            sum(columns[:, 3 * c + d : 3 * c + d + 1] * parts[d] for d in range(3))
            + columns[:, 9 + c : 10 + c]
            for c in range(3)
        ],
        axis=1,
    )


def fold(places):
    first, second, third = (places[:, LANES * c : LANES * (c + 1)] for c in range(3))
    low = iota((1, LANES), 1) < LANES // 2
    return jnp.concatenate([jnp.where(low, first, second), jnp.where(low, third, 0.0)], axis=1)


def head_of_fold(count):
    lane = iota((HEADS, 2 * LANES), 1)
    owner = lane % (LANES // 2) // count == iota((HEADS, 2 * LANES), 0)
    return (owner & (lane < 3 * LANES // 2)).astype(jnp.float32)


def head_of_lane(count):
    lane = iota((HEADS, 3 * LANES), 1) % LANES
    return (lane // count == iota((HEADS, 3 * LANES), 0)).astype(jnp.float32)


def attend_kernel(
    n_pb,
    n_ka,
    *refs,
):
    sources, refs = refs[:LOADS], refs[LOADS:]
    (states_out, pair_s, hidden_s), refs = refs[:3], refs[3:]
    targets, refs = refs[:LOADS], refs[LOADS:]
    (
        node,
        frames,
        chain,
        index,
        mask,
        relpos,
        edge_s,
        bias_rows_s,
        first,
        wq,
        point_query,
        point_key,
        point_value,
        perm_qk,
        perm_v,
        gamma,
        wk,
        wv,
        scales,
        ow,
    ) = targets
    (
        x_send,
        f_send,
        x_keys,
        f_keys,
        bias_s,
        work_s,
        stats_send,
        stats_recv,
        part_send,
        part_recv,
        columns_s,
        node_s,
        mine,
        load_sem,
            x_send_sem,
        x_recv_sem,
        f_send_sem,
        f_recv_sem,
        s_send_sem,
        s_recv_sem,
        p_send_sem,
        p_recv_sem,
        g_send_sem,
        g_recv_sem,
        h_send_sem,
        h_recv_sem,
    ) = refs
    rows, keys, channels = edge_s.shape
    count = chain.shape[1]
    part = rows // n_ka
    per = n_pb // n_ka
    row, col = lax.axis_index("pb"), lax.axis_index("ka")
    along_pb = [{"pb": lax.rem(row + d, n_pb)} for d in range(1, n_pb)]
    others = [lax.rem(col + d, n_ka) for d in range(1, n_ka)]
    along_ka = [{"ka": other} for other in others]

    barrier = pltpu.get_barrier_semaphore()
    for peer in along_pb + along_ka:
        pl.semaphore_signal(barrier, inc=1, device_id=peer, device_id_type=MESH)
    loads = [
        pltpu.make_async_copy(source, target, load_sem.at[k])
        for k, (source, target) in enumerate(zip(sources, targets))
    ]
    for load in loads:
        load.start()
    for load in loads[:6]:
        load.wait()

    x_send[...] = node[...].astype(jnp.bfloat16)
    f_send[...] = frames[...].astype(jnp.bfloat16)

    code = chain[...].astype(jnp.float32) * CHAIN_STEP + index[...].astype(jnp.float32)
    code = jnp.broadcast_to(code, (8, count))
    at_row = iota((count, LANES), 0) == row * rows + iota((count, LANES), 1)
    row_code = dot(code, at_row.astype(jnp.float32), precision=HIGHEST)[0:1]
    at_key = iota((keys, count), 1) == col * keys + iota((keys, count), 0)
    key_code = contract(at_key.astype(jnp.float32), code, 1, 1, precision=HIGHEST)[:, 0:1]
    reach = (RELBINS - 2) // 2
    gap = row_code - key_code
    bins = jnp.where(
        jnp.abs(gap) < CHAIN_STEP / 2, jnp.clip(gap, -reach, reach) + reach, RELBINS - 1.0
    )
    table = relpos[...]
    high = table.astype(jnp.bfloat16)
    low = (table - high.astype(jnp.float32)).astype(jnp.bfloat16)
    table = jnp.concatenate([high, low], axis=1)
    bin_lane = iota((keys, RELBINS), 1).astype(jnp.float32)
    for load in loads[6:8]:
        load.wait()
    bias_rows = bias_rows_s[...]

    def pair_rows(start, size):
        onehot = jnp.concatenate(
            [
                jnp.where(bins[:, i : i + 1] == bin_lane, 1.0, 0.0).astype(jnp.bfloat16)
                for i in range(start, start + size)
            ],
            axis=0,
        )
        relative = dot(onehot, table)
        relative = relative[:, :channels] + relative[:, channels:]
        values = edge_s[start : start + size].astype(jnp.float32).reshape(size * keys, channels)
        values = (values + relative).astype(jnp.bfloat16)
        pair_s[start : start + size] = values.reshape(size, keys, channels)
        for i in range(size):
            bias_s[(start + i) * HEADS : (start + i + 1) * HEADS, :] = contract(
                bias_rows, values[i * keys : (i + 1) * keys], 1, 1
            )

    group = 8
    starts = list(range(0, rows, group))

    pl.semaphore_wait(barrier, len(along_pb) + len(along_ka))
    for slot in range(per):

        @pl.when(row == col * per + slot)
        def _():
            copies = []
            for d, peer in enumerate(along_pb):
                copies.append(
                    pltpu.make_async_remote_copy(
                        src_ref=x_send,
                        dst_ref=x_keys.at[slot],
                        send_sem=x_send_sem.at[d],
                        recv_sem=x_recv_sem.at[slot],
                        device_id=peer,
                        device_id_type=MESH,
                    )
                )
                copies.append(
                    pltpu.make_async_remote_copy(
                        src_ref=f_send,
                        dst_ref=f_keys.at[slot],
                        send_sem=f_send_sem.at[d],
                        recv_sem=f_recv_sem.at[slot],
                        device_id=peer,
                        device_id_type=MESH,
                    )
                )
            for copy in copies:
                copy.start()
            x_keys[slot] = x_send[...]
            f_keys[slot] = f_send[...]

    for start in starts:
        pair_rows(start, group)

    own_columns = frame_columns(frames[...])
    for a in range(n_ka):
        columns_s[a] = own_columns[a * part : (a + 1) * part]
        node_s[a] = node[a * part : (a + 1) * part, :]
    own = x_send[...]
    for load in loads[8:16]:
        load.wait()
    queries = dot(own, wq[...]).astype(jnp.bfloat16)
    spread = dot(perm_qk[...], point_query[...]).astype(jnp.bfloat16)
    query_places = fold(place(contract(own, spread, 1, 1), own_columns))
    spread_key = dot(perm_qk[...], point_key[...]).astype(jnp.bfloat16)
    spread_value = dot(perm_v[...], point_value[...]).astype(jnp.bfloat16)
    heads_qk = head_of_fold(QKP)
    by_head = (query_places[:, None, :] * heads_qk[None]).reshape(rows * HEADS, 2 * LANES)
    query_square = jnp.sum(by_head * by_head, axis=-1, keepdims=True)

    for slot in range(per):

        @pl.when(row != col * per + slot)
        def _():
            pltpu.make_async_remote_copy(
                src_ref=x_send,
                dst_ref=x_keys.at[slot],
                send_sem=x_send_sem.at[0],
                recv_sem=x_recv_sem.at[slot],
                device_id=along_pb[0],
                device_id_type=MESH,
            ).wait_recv()
            pltpu.make_async_remote_copy(
                src_ref=f_send,
                dst_ref=f_keys.at[slot],
                send_sem=f_send_sem.at[0],
                recv_sem=f_recv_sem.at[slot],
                device_id=along_pb[0],
                device_id_type=MESH,
            ).wait_recv()

    key_rows = jnp.concatenate([x_keys[slot] for slot in range(per)], axis=0)
    key_columns = jnp.concatenate([frame_columns(f_keys[slot].astype(jnp.float32)) for slot in range(per)], axis=0)
    key_places = fold(place(contract(key_rows, spread_key, 1, 1), key_columns))
    cross = contract(by_head, key_places, 1, 1, precision=HIGHEST)
    key_square = contract(heads_qk, key_places * key_places, 1, 1, precision=HIGHEST)
    loads[16].wait()
    key_vectors = dot(key_rows, wk[...]).astype(jnp.bfloat16)
    for head in range(HEADS):
        window = slice(head * HD, (head + 1) * HD)
        work_s[pl.ds(head, rows, stride=HEADS), :] = contract(
            queries[:, window], key_vectors[:, window], 1, 1
        )
    own_head = iota((HEADS, HEADS), 0) == iota((HEADS, HEADS), 1)
    gammas = jnp.sum(jnp.where(own_head, gamma[...], 0.0), axis=1, keepdims=True)
    gammas = gammas * math.sqrt(2.0 / (9.0 * QKP))
    distance = (cross - 0.5 * query_square).reshape(rows, HEADS, keys) - 0.5 * key_square[None]
    logits = math.sqrt(1.0 / 3.0) * (
        work_s[...].reshape(rows, HEADS, keys) * (1.0 / math.sqrt(HD))
        + bias_s[...].reshape(rows, HEADS, keys)
        + gammas[None] * distance
    )
    key_first = pl.multiple_of(col * keys, keys)
    valid = (mask[0:1, pl.ds(key_first, keys)] == 1)[None]
    masked = jnp.where(valid, logits, NEG_FILL)
    top = jnp.max(masked, axis=-1, keepdims=True)
    weights = jnp.where(valid, jnp.exp(masked - top), 0.0)
    total = jnp.sum(weights, axis=-1, keepdims=True)
    lanes = stats_send.shape[-1]
    at_lane = iota((rows, 1, lanes), 0) == iota((rows, 1, lanes), 2)
    stats_send[0] = jnp.sum(jnp.where(at_lane, top, 0.0), axis=0)
    stats_send[1] = jnp.sum(jnp.where(at_lane, total, 0.0), axis=0)
    stats = [
        pltpu.make_async_remote_copy(
            src_ref=stats_send,
            dst_ref=stats_recv.at[d],
            send_sem=s_send_sem.at[d],
            recv_sem=s_recv_sem.at[d],
            device_id=peer,
            device_id_type=MESH,
        )
        for d, peer in enumerate(along_ka)
    ]
    for copy in stats:
        copy.start()

    work_s[...] = weights.reshape(rows * HEADS, keys)
    rounded = weights.astype(jnp.bfloat16)
    loads[17].wait()
    value_vectors = dot(key_rows, wv[...]).astype(jnp.bfloat16)
    scalar = [
        dot(
            work_s[pl.ds(head, rows, stride=HEADS), :].astype(jnp.bfloat16),
            value_vectors[:, head * HD : (head + 1) * HD],
        )
        for head in range(HEADS)
    ]
    pair_out = jnp.stack([dot(rounded[i], pair_s[i]) for i in range(rows)], axis=0)
    value_places = place(contract(key_rows, spread_value, 1, 1), key_columns)
    heads_v = head_of_lane(VP)
    value_high = value_places.astype(jnp.bfloat16)
    value_low = (value_places - value_high.astype(jnp.float32)).astype(jnp.bfloat16)
    weight_high = rounded.reshape(rows * HEADS, keys)
    weight_low = (work_s[...] - weight_high.astype(jnp.float32)).astype(jnp.bfloat16)
    points = dot(weight_high, value_high) + (
        dot(weight_high, value_low) + dot(weight_low, value_high)
    )
    points = jnp.sum(points.reshape(rows, HEADS, 3 * LANES) * heads_v[None], axis=1)

    for copy in stats:
        copy.wait()
    highest = stats_send[0]
    for d in range(n_ka - 1):
        highest = jnp.maximum(highest, stats_recv[d, 0])
    share = jnp.exp(stats_send[0] - highest)
    whole = stats_send[1] * share
    for d in range(n_ka - 1):
        whole = whole + stats_recv[d, 1] * jnp.exp(stats_recv[d, 0] - highest)
    real_row = iota(whole.shape, 1) < rows
    share = jnp.where(real_row, share / jnp.where(real_row, whole, 1.0), 0.0)
    factor = jnp.sum(jnp.where(at_lane, share[None], 0.0), axis=-1, keepdims=True)
    bias_s[...] = jnp.broadcast_to(factor, (rows, HEADS, keys)).reshape(rows * HEADS, keys)
    work_s[...] = (pair_out * factor).reshape(rows * HEADS, channels)
    for load in loads[18:]:
        load.wait()
    features = []
    for head in range(HEADS):
        scale = bias_s[pl.ds(head, rows, stride=HEADS), :]
        for half in range(HD // LANES):
            features.append(scalar[head][:, half * LANES : (half + 1) * LANES] * scale)
    for head in range(HEADS):
        features.append(work_s[pl.ds(head, rows, stride=HEADS), :])
    features = jnp.concatenate([piece.astype(jnp.bfloat16) for piece in features], axis=1)
    partial = dot(features, ow[: features.shape[1], :])
    points = points * contract(share, heads_v, 0, 0, precision=HIGHEST)[:rows]
    partial = jnp.concatenate([partial, points], axis=1)
    for a in range(n_ka):
        part_send[a] = partial[a * part : (a + 1) * part].astype(jnp.bfloat16)
    parts = [
        pltpu.make_async_remote_copy(
            src_ref=part_send.at[other],
            dst_ref=part_recv.at[d],
            send_sem=p_send_sem.at[d],
            recv_sem=p_recv_sem.at[d],
            device_id={"ka": other},
            device_id_type=MESH,
        )
        for d, other in enumerate(others)
    ]
    for copy in parts:
        copy.start()

    def hidden_rows(start):
        pair = pair_s[start : start + group].reshape(group * keys, channels)
        values = dot(pair, first[...]).astype(jnp.bfloat16)
        hidden_s[start : start + group] = values.reshape(group, keys, EH)

    third = -(-len(starts) // 3)
    for start in starts[:third]:
        hidden_rows(start)
    value_base = HEADS * (HD + C_Z)
    point_weight = dot(perm_v[...], ow[value_base : value_base + HEADS * 3 * VP, :]).astype(
        jnp.bfloat16
    )
    for copy in parts:
        copy.wait()
    merged = part_send[col].astype(jnp.float32)
    for d in range(n_ka - 1):
        merged = merged + part_recv[d].astype(jnp.float32)
    columns = columns_s[col]
    moved = [
        merged[:, C_S + LANES * c : C_S + LANES * (c + 1)] - columns[:, 9 + c : 10 + c]
        for c in range(3)
    ]
    local = [
        sum(columns[:, 3 * c + d : 3 * c + d + 1] * moved[c] for c in range(3)) for d in range(3)
    ]
    lengths = jnp.sqrt(sum(piece * piece for piece in local) + 1e-08)
    local = jnp.concatenate([piece.astype(jnp.bfloat16) for piece in local], axis=1)
    length_weight = ow[value_base + HEADS * 3 * VP :, :]
    states = (
        node_s[col]
        + merged[:, :C_S]
        + dot(local, point_weight)
        + dot(lengths[:, : HEADS * VP].astype(jnp.bfloat16), length_weight)
    )
    mine[...] = layer_norm(states, scales[...]).astype(jnp.bfloat16)
    states_out[row, col] = mine[...]
    def partner(distance):
        other = row
        for bit in (1 << k for k in range(n_pb.bit_length() - 1)):
            if distance & bit:
                other = other + bit * (1 - 2 * lax.rem(lax.div(row, bit), 2))
        return other

    gathers = [
        pltpu.make_async_remote_copy(
            src_ref=mine,
            dst_ref=states_out.at[row, col],
            send_sem=g_send_sem.at[distance - 1],
            recv_sem=g_recv_sem.at[distance - 1],
            device_id={"pb": partner(distance)},
            device_id_type=MESH,
        )
        for distance in range(1, n_pb)
    ]
    for copy in reversed(gathers):
        copy.start()

    def forward(distance):
        source = partner(distance)
        copies = [
            pltpu.make_async_remote_copy(
                src_ref=states_out.at[source, col] if distance else mine,
                dst_ref=states_out.at[source, col],
                send_sem=h_send_sem.at[distance, d],
                recv_sem=h_recv_sem.at[distance, d],
                device_id=peer,
                device_id_type=MESH,
            )
            for d, peer in enumerate(along_ka)
        ]
        for copy in copies:
            copy.start()
        return copies

    spreads = forward(0)
    for start in starts[third:]:
        hidden_rows(start)
    for distance in range(1, n_pb):
        gathers[distance - 1].wait_recv()
        spreads += forward(distance)
    for copy in gathers:
        copy.wait_send()
    for slot in range(per):

        @pl.when(row == col * per + slot)
        def _():
            for d, peer in enumerate(along_pb):
                pltpu.make_async_remote_copy(
                    src_ref=x_send,
                    dst_ref=x_keys.at[slot],
                    send_sem=x_send_sem.at[d],
                    recv_sem=x_recv_sem.at[slot],
                    device_id=peer,
                    device_id_type=MESH,
                ).wait_send()
                pltpu.make_async_remote_copy(
                    src_ref=f_send,
                    dst_ref=f_keys.at[slot],
                    send_sem=f_send_sem.at[d],
                    recv_sem=f_recv_sem.at[slot],
                    device_id=peer,
                    device_id_type=MESH,
                ).wait_send()

    for copy in spreads:
        copy.wait()


def attend(n_pb, n_ka, *operands):
    frames, edge = operands[1], operands[6]
    rows, keys, channels = edge.shape
    part, per = rows // n_ka, n_pb // n_ka
    lanes = -(-rows // LANES) * LANES
    bf16, f32 = jnp.bfloat16, jnp.float32
    dma = pltpu.SemaphoreType.DMA
    return pl.pallas_call(
        functools.partial(attend_kernel, n_pb, n_ka),
        out_shape=(
            jax.ShapeDtypeStruct((n_pb, n_ka, part, C_S), bf16),
            jax.ShapeDtypeStruct(edge.shape, bf16),
            jax.ShapeDtypeStruct((rows, keys, EH), bf16),
        ),
        in_specs=[HBM] * len(operands),
        out_specs=(VMEM,) * 3,
        scratch_shapes=[
            *[pltpu.VMEM(array.shape, array.dtype) for array in operands],
            pltpu.VMEM((rows, C_S), bf16),
            pltpu.VMEM(frames.shape, bf16),
            pltpu.VMEM((per, rows, C_S), bf16),
            pltpu.VMEM((per,) + frames.shape, bf16),
            pltpu.VMEM((rows * HEADS, keys), f32),
            pltpu.VMEM((rows * HEADS, keys), f32),
            pltpu.VMEM((2, HEADS, lanes), f32),
            pltpu.VMEM((n_ka - 1, 2, HEADS, lanes), f32),
            pltpu.VMEM((n_ka, part, C_S + 3 * LANES), bf16),
            pltpu.VMEM((n_ka - 1, part, C_S + 3 * LANES), bf16),
            pltpu.VMEM((n_ka, part, LANES), f32),
            pltpu.VMEM((n_ka, part, C_S), f32),
            pltpu.VMEM((part, C_S), bf16),
            dma((len(operands),)),
            dma((n_pb - 1,)),
            dma((per,)),
            dma((n_pb - 1,)),
            dma((per,)),
            dma((n_ka - 1,)),
            dma((n_ka - 1,)),
            dma((n_ka - 1,)),
            dma((n_ka - 1,)),
            dma((n_pb - 1,)),
            dma((n_pb - 1,)),
            dma((n_pb, n_ka - 1)),
            dma((n_pb, n_ka - 1)),
        ],
        compiler_params=pltpu.CompilerParams(
            collective_id=0, has_side_effects=True, vmem_limit_bytes=28 << 20
        ),
    )(*[pltpu.with_memory_space_constraint(array, pltpu.HBM) for array in operands])


def encoder_rows(states, keys, values, fill, project, output, expand, shrink, scales):
    queries = dot(states.astype(jnp.bfloat16), project[:, :C_S]).astype(
        jnp.bfloat16
    ) * jnp.asarray(1.0 / math.sqrt(TF_HD), jnp.bfloat16)
    owner = iota((1, C_S), 1) // TF_HD
    context = []
    for half in range(C_S // LANES):
        mixed = None
        for head in range(half * LANES // TF_HD, (half + 1) * LANES // TF_HD):
            only = jnp.where(owner == head, 1.0, 0.0).astype(jnp.bfloat16)
            scores = contract(queries * only, keys, 1, 1) + fill
            weights = jnp.exp(scores - jnp.max(scores, axis=-1, keepdims=True))
            sums = dot(weights.astype(jnp.bfloat16), values[head])
            totals = sums[:, (1 - half) * LANES : (2 - half) * LANES]
            sums = sums[:, half * LANES : (half + 1) * LANES] / totals
            mine = owner[:, half * LANES : (half + 1) * LANES] == head
            mixed = sums if mixed is None else jnp.where(mine, sums, mixed)
        context.append(mixed.astype(jnp.bfloat16))
    context = jnp.concatenate(context, axis=1)
    middle = layer_norm(states + dot(context, output), scales[0:1])
    hidden = jnp.maximum(dot(middle.astype(jnp.bfloat16), expand), 0.0).astype(jnp.bfloat16)
    return layer_norm(middle + dot(hidden, shrink), scales[1:2])


def update_frames(states, frames, frame_weight):
    update = contract(frame_weight, states, 1, 1, precision=HIGHEST)
    x, y, z = update[0:1], update[1:2], update[2:3]
    length = jnp.sqrt(1.0 + x * x + y * y + z * z)
    w, x, y, z = 1.0 / length, x / length, y / length, z / length
    turn = (
        (w * w + x * x - y * y - z * z, 2.0 * (x * y - w * z), 2.0 * (x * z + w * y)),
        (2.0 * (x * y + w * z), w * w - x * x + y * y - z * z, 2.0 * (y * z - w * x)),
        (2.0 * (x * z - w * y), 2.0 * (y * z + w * x), w * w - x * x - y * y + z * z),
    )
    old = [frames[k : k + 1] for k in range(12)]
    rotation = [
        sum(old[3 * c + d] * turn[d][e] for d in range(3)) for c in range(3) for e in range(3)
    ]
    offset = [
        sum(old[3 * c + d] * update[3 + d : 4 + d] for d in range(3)) + old[9 + c]
        for c in range(3)
    ]
    return jnp.concatenate(rotation + offset, axis=0)


def finish_kernel(
    n_ka,
    hidden_ref,
    pair_ref,
    states_ref,
    mask,
    frames,
    project,
    output,
    expand,
    shrink,
    scales,
    frame_weight,
    to_edge,
    second,
    third,
    biases,
    edge_scale,
    node_out,
    frames_out,
    edges_out,
    row_part,
    key_part,
    live_row,
    live_key,
    states_s,
    enc_keys,
    enc_values,
    second_tail,
    third_tail,
):
    step, keys, width = pair_ref.shape
    rows = node_out.shape[0]
    count = states_ref.shape[0]
    turn = pl.program_id(0)

    @pl.when(turn == 0)
    def _():
        row_first = pl.multiple_of(lax.axis_index("pb") * rows, rows)
        key_first = pl.multiple_of(lax.axis_index("ka") * keys, keys)
        fill = jnp.where(mask[...] == 1, 0.0, NEG_FILL)
        live = (mask[...] == 1).astype(jnp.bfloat16)
        live = jnp.broadcast_to(live, (16, count))
        at_row = (iota((rows, count), 1) == row_first + iota((rows, count), 0)).astype(jnp.bfloat16)
        at_key = (iota((keys, count), 1) == key_first + iota((keys, count), 0)).astype(jnp.bfloat16)
        live_row[...] = jnp.broadcast_to(contract(at_row, live, 1, 1)[:, 0:1], live_row.shape)
        live_key[...] = jnp.broadcast_to(contract(at_key, live, 1, 1)[:, 0:1], live_key.shape)

        def attended(states, layer):
            both = dot(states.astype(jnp.bfloat16), project[layer][:, C_S:]).astype(jnp.bfloat16)
            enc_keys[...] = both[:, :C_S]
            owner = iota((1, C_S), 1) // TF_HD
            for head in range(C_S // TF_HD):
                values = jnp.where(owner == head, both[:, C_S:].astype(jnp.float32), 1.0)
                enc_values[head] = values.astype(jnp.bfloat16)

        def apply(states, layer):
            return encoder_rows(
                states,
                enc_keys[...],
                enc_values,
                fill,
                project[layer],
                output[layer],
                expand[layer],
                shrink[layer],
                scales[layer],
            )

        attended(states_ref[...], 0)
        chunk = math.gcd(count, 512)
        for start in range(0, count, chunk):
            window = slice(start, start + chunk)
            states_s[window, :] = apply(states_ref[window, :].astype(jnp.float32), 0)
        attended(states_s[...], 1)
        both = jnp.concatenate(
            [states_s[pl.ds(row_first, rows), :], states_s[pl.ds(key_first, keys), :]], axis=0
        )
        final = apply(both, 1)
        node_out[...] = final[:rows]
        row_part[...] = dot(final[:rows].astype(jnp.bfloat16), to_edge[:, :EH])
        key_part[...] = dot(final[rows:].astype(jnp.bfloat16), to_edge[:, EH:]) + biases[0:1]
        wide = EH - LANES
        zeros = jnp.zeros((LANES, LANES), jnp.bfloat16)
        for target, block in (
            (second_tail, second[wide:, wide:]),
            (third_tail, third[wide:, :]),
        ):
            target[...] = jnp.concatenate(
                [
                    jnp.concatenate([block, zeros], axis=1),
                    jnp.concatenate([zeros, block], axis=1),
                ],
                axis=0,
            )
        frames_out[...] = update_frames(final[:rows], frames[...], frame_weight[...])

    window = pl.ds(pl.multiple_of(turn * step, step), step)
    pair = pair_ref[...].reshape(step * keys, width)
    hidden = hidden_ref[...].astype(jnp.float32)
    hidden = hidden + row_part[window, :][:, None, :] + key_part[...][None]
    hidden = jnp.maximum(hidden, 0.0).astype(jnp.bfloat16).reshape(step * keys, -1)
    wide = EH - LANES

    def tail(values, weights):
        half = values.shape[0] // 2
        both = jnp.concatenate([values[:half], values[half:]], axis=1)
        both = dot(both, weights)
        return jnp.concatenate([both[:, :LANES], both[:, LANES:]], axis=0)

    middle = dot(hidden, second[:, :wide]) + biases[1:2, :wide]
    middle = jnp.maximum(middle, 0.0).astype(jnp.bfloat16)
    rest = dot(hidden[:, :wide], second[:wide, wide:]) + tail(hidden[:, wide:], second_tail[...])
    rest = jnp.maximum(rest + biases[1:2, wide:], 0.0).astype(jnp.bfloat16)
    result = pair.astype(jnp.float32) + dot(middle, third[:wide, :]) + tail(rest, third_tail[...])
    normed = layer_norm(result, edge_scale[...]).reshape(step, keys, width)
    live = live_row[window, :][:, None, :] * live_key[...][None]
    edges_out[...] = (normed * live).astype(edges_out.dtype)


def finish(n_ka, hidden, pair, states, *rest):
    rows, keys, width = pair.shape
    frames = rest[1]
    step = math.gcd(rows, 16)
    count = states.shape[0]

    def whole(array):
        return pl.BlockSpec(
            array.shape, lambda i: (0,) * len(array.shape), pipeline_mode=pl.Buffered(1)
        )

    outs = (
        jax.ShapeDtypeStruct((rows, C_S), jnp.float32),
        jax.ShapeDtypeStruct(frames.shape, jnp.float32),
        jax.ShapeDtypeStruct(pair.shape, jnp.bfloat16),
    )
    return pl.pallas_call(
        functools.partial(finish_kernel, n_ka),
        grid=(rows // step,),
        out_shape=outs,
        in_specs=[
            pl.BlockSpec((step, keys, EH), lambda i: (i, 0, 0)),
            pl.BlockSpec((step, keys, width), lambda i: (i, 0, 0)),
        ]
        + [whole(array) for array in (states, *rest)],
        out_specs=(
            pl.BlockSpec((rows, C_S), lambda i: (0, 0)),
            pl.BlockSpec(frames.shape, lambda i: (0, 0)),
            pl.BlockSpec((step, keys, width), lambda i: (i, 0, 0)),
        ),
        scratch_shapes=[
            pltpu.VMEM((rows, EH), jnp.float32),
            pltpu.VMEM((keys, EH), jnp.float32),
            pltpu.VMEM((rows, width), jnp.float32),
            pltpu.VMEM((keys, width), jnp.float32),
            pltpu.VMEM((count, C_S), jnp.float32),
            pltpu.VMEM((count, C_S), jnp.bfloat16),
            pltpu.VMEM((C_S // TF_HD, count, C_S), jnp.bfloat16),
            pltpu.VMEM((2 * LANES, 2 * LANES), jnp.bfloat16),
            pltpu.VMEM((2 * LANES, 2 * LANES), jnp.bfloat16),
        ],
        compiler_params=pltpu.CompilerParams(vmem_limit_bytes=28 << 20),
    )(hidden, pair, states, *rest)


def on_device(
    node_states,
    frames,
    edge_states,
    chain_number,
    residue_index,
    padding_mask,
    query_weight,
    key_weight,
    value_weight,
    point_query,
    point_key,
    point_value,
    bias_weight,
    point_gamma,
    relpos_table,
    output_weight,
    attention_scales,
    layer_project,
    layer_output,
    layer_expand,
    layer_shrink,
    layer_scales,
    frame_weight,
    node_to_edge,
    edge_first,
    edge_second,
    edge_third,
    edge_biases,
    edge_scales,
):
    n_pb, n_ka = lax.axis_size("pb"), lax.axis_size("ka")
    mask = padding_mask[None]
    perm_qk, perm_v = (jnp.asarray(by_component(k).T, jnp.bfloat16) for k in (QKP, VP))
    states, pair, hidden = attend(
        n_pb,
        n_ka,
        node_states,
        frames,
        chain_number[None],
        residue_index[None],
        mask,
        relpos_table,
        edge_states,
        jnp.transpose(bias_weight),
        edge_first,
        query_weight,
        jnp.transpose(point_query),
        jnp.transpose(point_key),
        jnp.transpose(point_value),
        perm_qk,
        perm_v,
        point_gamma[None],
        key_weight,
        value_weight,
        attention_scales[None],
        output_weight,
    )
    return finish(
        n_ka,
        hidden,
        pair,
        states.reshape(-1, C_S),
        mask,
        frames,
        layer_project,
        layer_output,
        layer_expand,
        layer_shrink,
        layer_scales,
        jnp.transpose(frame_weight),
        node_to_edge,
        edge_second,
        edge_third,
        edge_biases,
        edge_scales[None],
    )


def solution(mesh):
    placed = [P()] * 29
    placed[:3] = [P("pb", None), P(None, "pb"), P("pb", "ka", None)]
    return jax.shard_map(
        on_device,
        mesh=mesh,
        in_specs=tuple(placed),
        out_specs=(P("pb", None), P(None, "pb"), P("pb", "ka", None)),
        check_vma=False,
    )
```
